256 devices in a mesh: strip: 16 (over z, y_hi), chan: 16 (over y_lo, x, core).
Axes of the slice: x: 4, y: 4 (y_hi: 2, y_lo: 2; y = y_hi * 2 + y_lo), z: 8, core: 2. Of those that a mesh axis runs over, the one named last changes fastest.
Arguments:
- grid: bfloat16 [2, 64, 1024, 1024], P(None, 'chan', 'strip'), may hold values from -6 to 6
- model_image: float32 [64, 1024, 1024], P('chan', 'strip'), may hold values from -160 to 160
- step_size: float32 [64], P('chan'), may hold values from 0.5 to 1.5
- highpass: float32 [3, 4], replicated, may hold values from -1.4 to 1.4
- shrinkage: float32 [16], P('strip'), may hold values from 0.1 to 0.5
Outputs:
- updated: float32 [64, 1024, 1024], P('chan', 'strip')
The draws below stay inside these ranges and needn't reach their ends.
All inputs are finite; a program needn't handle non-finite values.
Results may differ from the reference program's by a relative error of at most 0.0019.
Values may be sent and summed in bfloat16 or wider, within the bound.
A program may use at most 64 MiB of HBM per device.

```python
import math
import jax
import jax.numpy as jnp
from jax import lax

CH = 64
IMG = 1024
LEVELS = 3
FILT = 4
NS_ITERS = 5
FACET_ROWS = 64
FACETS = 16


def draw_model_image(key, part):
    subkeys = jax.random.split(jax.random.fold_in(key, 17), 6)
    log_low = math.log(0.3)
    log_high = math.log(3.0)
    row_scale = jnp.exp(jax.random.uniform(subkeys[0], (CH, IMG, 1), jnp.float32, log_low, log_high))
    col_scale = jnp.exp(jax.random.uniform(subkeys[1], (CH, 1, IMG), jnp.float32, log_low, log_high))
    region_side = IMG // 16
    region_scale = jnp.exp(jax.random.uniform(subkeys[2], (CH, 16, 16), jnp.float32, log_low, log_high))
    region_full = jnp.repeat(jnp.repeat(region_scale, region_side, axis=1), region_side, axis=2)
    row_index = jnp.arange(IMG, dtype=jnp.int32)
    row_ramp = 1.0 + (row_index % FACET_ROWS).astype(jnp.float32) / FACET_ROWS
    col_ramp = 1.0 + row_index.astype(jnp.float32) / IMG
    noise_field = jnp.clip(jax.random.normal(subkeys[3], (CH, IMG, IMG), jnp.float32), -4.0, 4.0)
    mixing = 0.6
    shared = jnp.clip(jax.random.normal(subkeys[4], (1, IMG, IMG), jnp.float32), -4.0, 4.0)
    loading = jnp.clip(jax.random.normal(subkeys[5], (CH, 16, 16), jnp.float32), -4.0, 4.0)
    loading_full = jnp.repeat(jnp.repeat(loading, region_side, axis=1), region_side, axis=2)
    values = 0.3 * region_full * row_scale * col_scale * row_ramp[None, :, None] * col_ramp[None, None, :] * noise_field
    return values + mixing * shared * loading_full


def block_levels(rng, extent, pieces, smallest, top_value):
    def one(dim, blocks):
        heights = jax.random.uniform(jax.random.fold_in(jax.random.fold_in(rng, 6), dim), (blocks,), jnp.float32, smallest / len(pieces), top_value / len(pieces))
        return jnp.repeat(jnp.exp(heights), extent[dim] // blocks).reshape((-1,) + (1,) * (len(extent) - dim - 1))

    factor_of = one(*pieces[0])
    for cut in pieces[1:]:
        factor_of = factor_of * one(*cut)
    return factor_of


def noise(stream_key, dims, deviation, reach, pieces=(), kind=jnp.bfloat16):
    array = deviation * jax.random.normal(stream_key, dims, jnp.float32)
    if pieces:
        array = array * block_levels(stream_key, dims, pieces, -0.22, 0.18)
    return jnp.clip(array, -reach, reach).astype(kind)


def setup_inputs(seed: int = 0) -> dict:
    splits = jax.random.split(jax.random.key(seed), 6)
    grid = noise(splits[0], (2, CH, IMG, IMG), 1.0, 6.0, ((1, 16), (2, 16)))
    model_image = draw_model_image(jax.random.fold_in(splits[5], 71), 0)
    step_size = jnp.clip(jnp.exp(math.log(1.5) - 1.0986123 * jax.random.uniform(splits[2], (CH,), jnp.float32) ** block_levels(splits[2], (CH,), ((0, 16),), -0.2, 0.2)), 0.5, 1.5)
    highpass = noise(splits[3], (LEVELS, FILT), 0.35, 1.4, (), jnp.float32)
    shrinkage = jnp.clip(jnp.exp(math.log(0.5) - 1.609438 * jax.random.uniform(splits[4], (FACETS,), jnp.float32) ** block_levels(splits[4], (FACETS,), ((0, 16),), -0.2, 0.2)), 0.1, 0.5)
    return dict(grid=grid, model_image=model_image, step_size=step_size, highpass=highpass, shrinkage=shrinkage)


def make_tables():
    indices = jnp.arange(IMG, dtype=jnp.int32)
    products = indices[:, None] * indices[None, :] % IMG
    phases = products.astype(jnp.float32) * (2.0 * 3.141592653589793 / IMG)
    unit_scale = float(IMG) ** (-0.5)
    cosine = (jnp.cos(phases) * unit_scale).astype(jnp.bfloat16)
    sine_table = (jnp.sin(phases) * unit_scale).astype(jnp.bfloat16)
    return (cosine, sine_table)

def dirty_channel(cosine, sine_table, plane):
    real_part = plane[0]
    imag_part = plane[1]
    half_real = jnp.dot(real_part, cosine, preferred_element_type=jnp.float32) - jnp.dot(imag_part, sine_table, preferred_element_type=jnp.float32)
    half_imag = jnp.dot(real_part, sine_table, preferred_element_type=jnp.float32) + jnp.dot(imag_part, cosine, preferred_element_type=jnp.float32)
    half_real = half_real.astype(jnp.bfloat16)
    half_imag = half_imag.astype(jnp.bfloat16)
    return jnp.dot(half_real.T, cosine, preferred_element_type=jnp.float32) - jnp.dot(half_imag.T, sine_table, preferred_element_type=jnp.float32)

def wavelet_gradient(image, highpass):
    running = jnp.zeros(image.shape, jnp.float32)
    half_taps = FILT // 2
    for level_idx in range(LEVELS):
        dilation = 2 ** level_idx
        reach_rows = half_taps * dilation
        padded = jnp.pad(image, ((0, 0), (reach_rows, reach_rows), (0, 0)))
        detail = jnp.zeros(image.shape, jnp.float32)
        for tap_index in range(FILT):
            offset = (tap_index - half_taps) * dilation
            detail = detail + highpass[level_idx, tap_index] * padded[:, reach_rows + offset:reach_rows + offset + IMG, :]
        padded = jnp.pad(detail, ((0, 0), (reach_rows, reach_rows), (0, 0)))
        for tap_index in range(FILT):
            offset = (tap_index - half_taps) * dilation
            running = running + highpass[level_idx, tap_index] * padded[:, reach_rows - offset:reach_rows - offset + IMG, :]
    return running

def newton_schulz(gram_sum):
    frob_norm = jnp.sqrt(jnp.sum(gram_sum * gram_sum))
    identity = jnp.eye(gram_sum.shape[0], dtype=jnp.float32)
    current = gram_sum / frob_norm
    inverse = identity
    for iteration in range(NS_ITERS):
        middle = 0.5 * (3.0 * identity - jnp.dot(inverse, current, precision=lax.Precision.HIGHEST))
        current = jnp.dot(current, middle, precision=lax.Precision.HIGHEST)
        inverse = jnp.dot(middle, inverse, precision=lax.Precision.HIGHEST)
    return (inverse, frob_norm)

def facet_prox(packed):
    pixels, shrink_one = packed
    gram_sum = jnp.dot(pixels, pixels.T, precision=lax.Precision.HIGHEST)
    inverse, frob_norm = newton_schulz(gram_sum)
    polar = jnp.sqrt(pixels.shape[1] / frob_norm) * jnp.dot(inverse.T, pixels, precision=lax.Precision.HIGHEST)
    return pixels - shrink_one * polar

def reference(grid, model_image, step_size, highpass, shrinkage):
    cosine, sine_table = make_tables()
    planes = jnp.moveaxis(grid, 1, 0)
    dirty_image = lax.map(lambda plane: dirty_channel(cosine, sine_table, plane), planes)
    wavelet_grad = wavelet_gradient(model_image, highpass)
    moved = model_image + step_size[:, None, None] * (dirty_image - wavelet_grad)
    blocks = moved.reshape(CH, FACETS, FACET_ROWS * IMG).transpose(1, 0, 2)
    results = lax.map(facet_prox, (blocks, shrinkage))
    return results.transpose(1, 0, 2).reshape(CH, IMG, IMG)
```

```python
import functools

import jax
import jax.numpy as jnp
import numpy as np
from jax import lax
from jax.experimental import pallas as pl
from jax.experimental.pallas import tpu as pltpu
from jax.sharding import PartitionSpec as P

NS_ITERS = 5
MESH = pl.DeviceIdType.MESH
HALO = 16
NT = (((1,), (1,)), ((), ()))
F32 = jnp.float32
BF16 = jnp.bfloat16


def make_tables(side, strips):
    index = np.arange(side, dtype=np.int64)
    phases = (index[:, None] * index[None, :] % side) * (2.0 * np.pi / side)
    scale = float(side) ** -0.5
    both = np.stack((np.cos(phases), np.sin(phases))) * scale
    return jnp.asarray(both.astype(np.float32)).astype(BF16).reshape(2, strips, side // strips, side)


def exact_dot(a, b):
    return jnp.dot(a, b, precision=lax.Precision.HIGHEST, preferred_element_type=F32)


def kernel(
    strips, chans, tab, grid, model, step, taps, shrink, out,
    tabn, pairs, g_v, m_v, xc, xs, send_a, recv_a, ext_hi, ext_lo, base, send_b, recv_b, x, grecv,
    stage, send_c, polar,
    load_sem, tab_sem, a_send, a_recv, b_send, b_recv, g_send, g_recv, c_send, c_recv, h_send, h_recv,
):
    me_s = lax.axis_index("strip")
    me_c = lax.axis_index("chan")
    local, rows, side = base.shape
    wide = 2 * rows
    half = rows // 2
    lb = me_c // 2
    rh = lax.rem(me_c, 2)
    levels, filt = taps.shape

    def strip_peer(d):
        return lax.rem(me_s + d + strips, strips)

    def chan_peer(d):
        return lax.rem(me_c + d + chans, chans)

    load_grid = pltpu.make_async_copy(grid, g_v, load_sem.at[0])
    load_grid.start()
    load_model = pltpu.make_async_copy(model, m_v, load_sem.at[1])
    load_model.start()
    nblk = strips // 4
    first = me_s // 4

    def block_of(i):
        return lax.rem(first + i, nblk) * 4

    def tab_copy(i, r):
        rows_of = pl.ds(block_of(i), 4)
        return pltpu.make_async_copy(tab.at[r, rows_of], tabn.at[r, rows_of], tab_sem.at[i, r])

    for i in range(nblk):
        for r in range(2):
            tab_copy(i, r).start()
    load_pairs = [pltpu.make_async_copy(tab.at[r], pairs.at[:, r], load_sem.at[2 + r]) for r in range(2)]
    for cp in load_pairs:
        cp.start()

    barrier = pltpu.get_barrier_semaphore()

    @pl.loop(1, strips)
    def _(d):
        pl.semaphore_signal(barrier, inc=1, device_id=(strip_peer(d), me_c), device_id_type=MESH)

    @pl.loop(1, chans)
    def _(d):
        pl.semaphore_signal(barrier, inc=1, device_id=(me_s, chan_peer(d)), device_id_type=MESH)

    load_model.wait()
    ext_hi[:, rows + 2 * HALO :, :] = jnp.zeros((local, 128 - rows - 2 * HALO, side), BF16)
    ext_lo[:, :HALO, :] = jnp.zeros((local, HALO, side), BF16)
    ext_lo[:, rows + HALO :, :] = jnp.zeros((local, 128 - rows - HALO, side), BF16)
    for c in range(local):
        value = m_v[c]
        top = value.astype(BF16)
        ext_hi[c, HALO : HALO + rows, :] = top
        ext_lo[c, HALO : HALO + rows, :] = (value - top.astype(F32)).astype(BF16)

    load_grid.wait()
    for c in range(local):
        re = g_v[0, c]
        im = -g_v[1, c]
        xc[c * wide : c * wide + rows, :] = re
        xc[c * wide + rows : (c + 1) * wide, :] = im
        xs[c * wide : c * wide + rows, :] = im
        xs[c * wide + rows : (c + 1) * wide, :] = -re

    pl.semaphore_wait(barrier, strips - 1 + chans - 1)

    halo_copies = [
        pltpu.make_async_remote_copy(
            src_ref=ext_hi.at[:, rows : rows + HALO, :], dst_ref=ext_hi.at[:, 0:HALO, :],
            send_sem=h_send.at[0], recv_sem=h_recv.at[0],
            device_id=(strip_peer(1), me_c), device_id_type=MESH,
        ),
        pltpu.make_async_remote_copy(
            src_ref=ext_hi.at[:, HALO : 2 * HALO, :], dst_ref=ext_hi.at[:, rows + HALO : rows + 2 * HALO, :],
            send_sem=h_send.at[1], recv_sem=h_recv.at[1],
            device_id=(strip_peer(-1), me_c), device_id_type=MESH,
        ),
    ]
    for cp in halo_copies:
        cp.start()

    def a_src(k, d):
        return send_a.at[pl.ds(pl.multiple_of(strip_peer(d) * rows, rows), rows), pl.ds(k * wide, wide)]

    def a_dst(k):
        return recv_a.at[k, :, pl.ds(pl.multiple_of(me_s * wide, wide), wide)]

    def a_remote(k, d):
        return pltpu.make_async_remote_copy(
            src_ref=a_src(k, d), dst_ref=a_dst(k), send_sem=a_send.at[k, d], recv_sem=a_recv.at[k, d],
            device_id=(strip_peer(d), me_c), device_id_type=MESH,
        )

    def a_local(k):
        return pltpu.make_async_copy(a_src(k, 0), a_dst(k), a_recv.at[k, 0])

    @pl.loop(0, nblk)
    def _(i):
        b = block_of(i)
        for r in range(2):
            tab_copy(i, r).wait()
        cos_rows = tabn[0, pl.ds(b, 4)].reshape(4 * rows, side)
        sin_rows = tabn[1, pl.ds(b, 4)].reshape(4 * rows, side)
        value = lax.dot_general(cos_rows, xc[...], NT, preferred_element_type=F32)
        value = value + lax.dot_general(sin_rows, xs[...], NT, preferred_element_type=F32)
        send_a[pl.ds(pl.multiple_of(b * rows, 4 * rows), 4 * rows), :] = value.astype(BF16)

        @pl.loop(0, 4)
        def _(t):
            d = lax.rem(b + t - me_s + strips, strips)

            @pl.when(d != 0)
            def _():
                a_remote(0, d).start()

            @pl.when(d == 0)
            def _():
                a_local(0).start()

    for k in range(1, local):
        a_local(k).start()

        @pl.loop(1, strips)
        def _(d):
            a_remote(k, d).start()

    row = lax.broadcasted_iota(jnp.int32, (rows, 128), 0)
    col = lax.broadcasted_iota(jnp.int32, (rows, 128), 1)
    shift = col - row - HALO
    total = strips * rows
    base_row = me_s * rows
    band = jnp.zeros((rows, 128), F32)
    for j in range(levels):
        dil = 2**j
        for k in range(filt):
            inner = jnp.zeros((rows, 128), F32)
            for q in range(filt):
                inner = inner + jnp.where(shift == (q - k) * dil, taps[j, q], 0.0)
            detail_row = base_row + row - (k - filt // 2) * dil
            ok = jnp.logical_and(detail_row >= 0, detail_row < total)
            band = band + jnp.where(ok, taps[j, k] * inner, 0.0)
    image_row = base_row + col - HALO
    band = jnp.where(jnp.logical_and(image_row >= 0, image_row < total), band, 0.0)
    band_hi = band.astype(BF16)
    band_lo = (band - band_hi.astype(F32)).astype(BF16)
    x[...] = jnp.zeros(x.shape, BF16)
    for cp in halo_copies:
        cp.wait_recv()
    for c in range(local):
        near = ext_hi[c]
        wav = jnp.dot(band_hi, near, preferred_element_type=F32)
        wav = wav + jnp.dot(band_hi, ext_lo[c], preferred_element_type=F32)
        wav = wav + jnp.dot(band_lo, near, preferred_element_type=F32)
        base[c] = m_v[c] - step[c] * wav

    for cp in load_pairs:
        cp.wait()

    def b_remote(k, d):
        peer = chan_peer(d)
        return pltpu.make_async_remote_copy(
            src_ref=send_b.at[
                k, pl.ds(pl.multiple_of(lax.rem(peer, 2) * half, half), half), pl.ds(pl.multiple_of(peer // 2 * 128, 128), 128)
            ],
            dst_ref=recv_b.at[k, me_c], send_sem=b_send.at[k, d], recv_sem=b_recv.at[k, d],
            device_id=(me_s, peer), device_id_type=MESH,
        )

    def b_local(k):
        return pltpu.make_async_copy(
            send_b.at[k, pl.ds(pl.multiple_of(rh * half, half), half), pl.ds(pl.multiple_of(lb * 128, 128), 128)],
            recv_b.at[k, me_c], b_recv.at[k, 0],
        )

    def arrive_a(k):
        a_local(k).wait()

        @pl.loop(1, strips)
        def _(d):
            a_remote(k, d).wait_recv()

        @pl.loop(0, side // 256)
        def _(n):
            cols = pl.ds(pl.multiple_of(n * 256, 256), 256)
            dirty = jnp.dot(
                recv_a[k], pairs[:, :, :, cols].reshape(strips * wide, 256), preferred_element_type=F32
            )
            value = base[k, :, cols] + step[k] * dirty
            base[k, :, cols] = value
            send_b[k, :, cols] = value.astype(BF16)

        b_local(k).start()

        @pl.loop(1, chans)
        def _(d):
            b_remote(k, d).start()

    def g_remote(k, d):
        return pltpu.make_async_remote_copy(
            src_ref=grecv.at[k, me_c], dst_ref=grecv.at[k, me_c], send_sem=g_send.at[k, d], recv_sem=g_recv.at[k, d],
            device_id=(me_s, chan_peer(d)), device_id_type=MESH,
        )

    def arrive_b(k):
        b_local(k).wait()

        @pl.loop(1, chans)
        def _(d):
            b_remote(k, d).wait_recv()

        stage[: chans * half, :] = recv_b[k].astype(F32).reshape(chans * half, 128)
        for m in range(half):
            x[k * chans : (k + 1) * chans, m * 128 : (m + 1) * 128] = stage[pl.ds(m, chans, stride=half), :].astype(BF16)
        part = lax.dot_general(x[k * chans : (k + 1) * chans, :], x[...], NT, preferred_element_type=F32)
        grecv[k, me_c] = part

        @pl.loop(1, chans)
        def _(d):
            g_remote(k, d).start()

    for k in range(local):
        arrive_a(k)
        if k:
            arrive_b(k - 1)
    arrive_b(local - 1)

    size = local * chans
    blocks = []
    for k in range(local):

        @pl.loop(1, chans)
        def _(d):
            g_remote(k, d).wait_recv()

        blocks.append(jnp.sum(grecv[k], axis=0))
    low = jnp.concatenate(blocks, axis=0)[:, :size]
    gi = lax.broadcasted_iota(jnp.int32, (size, size), 0)
    gj = lax.broadcasted_iota(jnp.int32, (size, size), 1)
    identity = jnp.where(gi == gj, 1.0, 0.0).astype(F32)
    strict = jnp.where(gi // chans > gj // chans, low, 0.0)
    upper = lax.dot_general(
        strict, identity, (((0,), (0,)), ((), ())), precision=lax.Precision.HIGHEST, preferred_element_type=F32
    )
    gram = low + upper
    square = jnp.sum(jnp.sum(gram * gram, axis=1, keepdims=True), axis=0, keepdims=True)
    frob = jnp.sqrt(square)
    current = gram / frob
    inverse = 0.5 * (3.0 * identity - current)
    current = exact_dot(current, inverse)
    for it in range(1, NS_ITERS):
        middle = 0.5 * (3.0 * identity - exact_dot(inverse, current))
        if it + 1 < NS_ITERS:
            current = exact_dot(current, middle)
        inverse = exact_dot(middle, inverse)
    factor = shrink[0] * jnp.sqrt(float(rows * side) / frob)
    mix = lax.dot_general(
        inverse, identity, (((0,), (0,)), ((), ())), precision=lax.Precision.HIGHEST, preferred_element_type=F32
    )
    mix = (factor * mix).astype(BF16)

    for q in range(half // 4):
        value = jnp.dot(mix, x[:size, q * 512 : (q + 1) * 512], preferred_element_type=F32)
        for t in range(4):
            stage[pl.ds(q * 4 + t, size, stride=half), :] = value[:, t * 128 : (t + 1) * 128]
    for k in range(local):
        span = chans * half
        send_c[:, k] = stage[k * span : (k + 1) * span, :].reshape(chans, half, 128).astype(BF16)

    def c_dst():
        return polar.at[:, pl.ds(pl.multiple_of(rh * half, half), half), pl.ds(pl.multiple_of(lb * 128, 128), 128)]

    def c_remote(d):
        peer = chan_peer(d)
        return pltpu.make_async_remote_copy(
            src_ref=send_c.at[peer], dst_ref=c_dst(), send_sem=c_send.at[d], recv_sem=c_recv.at[d],
            device_id=(me_s, peer), device_id_type=MESH,
        )

    own = pltpu.make_async_copy(send_c.at[me_c], c_dst(), c_recv.at[0])
    own.start()

    @pl.loop(1, chans)
    def _(d):
        c_remote(d).start()

    own.wait()

    @pl.loop(1, chans)
    def _(d):
        c_remote(d).wait_recv()

    for c in range(local):
        out[c] = base[c] - polar[c].astype(F32)

    for cp in halo_copies:
        cp.wait_send()
    for k in range(local):

        @pl.loop(1, strips)
        def _(d):
            a_remote(k, d).wait_send()

        @pl.loop(1, chans)
        def _(d):
            b_remote(k, d).wait_send()
            g_remote(k, d).wait_send()

    @pl.loop(1, chans)
    def _(d):
        c_remote(d).wait_send()


def solution(mesh):
    strips, chans = mesh.shape["strip"], mesh.shape["chan"]

    def step_fn(grid, model, step, taps, shrink):
        local, rows, side = model.shape
        wide = 2 * rows
        half = rows // 2
        tab = make_tables(side, strips)
        dma = pltpu.SemaphoreType.DMA
        anywhere = pl.BlockSpec(memory_space=pl.ANY)
        scalars = pl.BlockSpec(memory_space=pltpu.SMEM)
        return pl.pallas_call(
            functools.partial(kernel, strips, chans),
            out_shape=jax.ShapeDtypeStruct((local, rows, side), F32),
            in_specs=[anywhere, anywhere, anywhere, scalars, scalars, scalars],
            out_specs=pl.BlockSpec(memory_space=pltpu.VMEM),
            scratch_shapes=[
                pltpu.VMEM((2, strips, rows, side), BF16),
                pltpu.VMEM((strips, 2, rows, side), BF16),
                pltpu.VMEM((2, local, rows, side), BF16),
                pltpu.VMEM((local, rows, side), F32),
                pltpu.VMEM((local * wide, side), BF16),
                pltpu.VMEM((local * wide, side), BF16),
                pltpu.VMEM((side, local * wide), BF16),
                pltpu.VMEM((local, rows, strips * wide), BF16),
                pltpu.VMEM((local, 128, side), BF16),
                pltpu.VMEM((local, 128, side), BF16),
                pltpu.VMEM((local, rows, side), F32),
                pltpu.VMEM((local, rows, side), BF16),
                pltpu.VMEM((local, chans, half, 128), BF16),
                pltpu.VMEM((128, half * 128), BF16),
                pltpu.VMEM((local, chans, chans, 128), F32),
                pltpu.VMEM((local * chans * half, 128), F32),
                pltpu.VMEM((chans, local, half, 128), BF16),
                pltpu.VMEM((local, rows, side), BF16),
                dma((4,)), dma((strips // 4, 2)),
                dma((local, strips)), dma((local, strips)),
                dma((local, chans)), dma((local, chans)),
                dma((local, chans)), dma((local, chans)),
                dma((chans,)), dma((chans,)),
                dma((2,)), dma((2,)),
            ],
            compiler_params=pltpu.CompilerParams(
                collective_id=0, has_side_effects=True, vmem_limit_bytes=62 * 1024 * 1024
            ),
            name="imaging_step",
        )(tab, grid, model, step, taps, shrink)

    return jax.shard_map(
        step_fn,
        mesh=mesh,
        in_specs=(
            P(None, "chan", "strip", None),
            P("chan", "strip", None),
            P("chan"),
            P(),
            P("strip"),
        ),
        out_specs=P("chan", "strip", None),
        check_vma=False,
    )
```

```python
import functools

import jax
import jax.numpy as jnp
import numpy as np
from jax import lax
from jax.experimental import pallas as pl
from jax.experimental.pallas import tpu as pltpu
from jax.sharding import PartitionSpec as P

NS_ITERS = 5
MESH = pl.DeviceIdType.MESH
HALO = 16
NT = (((1,), (1,)), ((), ()))
F32 = jnp.float32
BF16 = jnp.bfloat16


def make_tables(side, strips):
    index = np.arange(side, dtype=np.int64)
    phases = (index[:, None] * index[None, :] % side) * (2.0 * np.pi / side)
    scale = float(side) ** -0.5
    both = np.stack((np.cos(phases), np.sin(phases))) * scale
    both = both.reshape(2, strips, side // strips, side).swapaxes(0, 1)
    return jnp.asarray(both.astype(np.float32).astype(BF16))


def exact_dot(a, b):
    return jnp.dot(a, b, precision=lax.Precision.HIGHEST, preferred_element_type=F32)


def kernel(
    strips, chans, tab, grid, model, step, taps, shrink, out,
    tb, g_v, m_v, xc, xs, send_a, recv_a, ext_hi, ext_lo, base, send_b, recv_b, x, grecv,
    stage, send_c, polar,
    load_sem, tab_sem, a_send, a_recv, b_send, b_recv, g_send, g_recv, c_send, c_recv, h_send, h_recv,
):
    me_s = lax.axis_index("strip")
    me_c = lax.axis_index("chan")
    local, rows, side = base.shape
    wide = 2 * rows
    half = rows // 2
    lb = me_c // 2
    rh = lax.rem(me_c, 2)
    levels, filt = taps.shape
    ring = strips // 2
    xring = chans // 4

    def slot_strip(j):
        q = j // 2
        dz = ring // 2 + ((q + 1) // 2) * (1 - 2 * lax.rem(q, 2))
        z = lax.rem(me_s // 2 - dz + 2 * ring, ring)
        return z * 2 + lax.rem(lax.rem(me_s, 2) + 1 - lax.rem(j, 2), 2)

    def partner_slot(j):
        q = j // 2
        inner = jnp.logical_and(q > 0, q < ring - 1)
        return j + jnp.where(inner, 2 * (2 * lax.rem(q, 2) - 1), 0)

    def chan_peer(j):
        q = j // 4
        dx = xring // 2 + ((q + 1) // 2) * (1 - 2 * lax.rem(q, 2))
        core = lax.rem(lax.rem(me_c, 2) + 1 - lax.rem(j, 2), 2)
        xpos = lax.rem(lax.rem(me_c // 2, xring) + dx + xring, xring)
        pair = lax.rem(me_c // (2 * xring) + 1 - lax.rem(j // 2, 2), 2)
        return pair * 2 * xring + xpos * 2 + core

    def strip_next(d):
        return lax.rem(me_s + d + strips, strips)

    barrier = pltpu.get_barrier_semaphore()

    @pl.loop(0, strips - 1)
    def _(j):
        pl.semaphore_signal(barrier, inc=1, device_id=(slot_strip(j), me_c), device_id_type=MESH)

    load_grid = pltpu.make_async_copy(grid, g_v, load_sem.at[0])
    load_grid.start()

    def tab_start(i):
        @pl.loop(4 * i, 4 * i + 4)
        def _(j):
            pltpu.make_async_copy(tab.at[slot_strip(j)], tb.at[j], tab_sem.at[i]).start()

    def tab_wait(i):
        part = tb.at[4 * i : 4 * i + 4]
        pltpu.make_async_copy(part, part, tab_sem.at[i]).wait()

    tab_start(0)

    @pl.loop(0, chans - 1)
    def _(j):
        pl.semaphore_signal(barrier, inc=1, device_id=(me_s, chan_peer(j)), device_id_type=MESH)

    nblk = strips // 4
    for i in range(1, nblk):
        tab_start(i)
    load_model = pltpu.make_async_copy(model, m_v, load_sem.at[1])
    load_model.start()

    load_grid.wait()
    for c in range(local):
        re = g_v[0, c]
        im = -g_v[1, c]
        xc[c * wide : c * wide + rows, :] = re
        xc[c * wide + rows : (c + 1) * wide, :] = im
        xs[c * wide : c * wide + rows, :] = im
        xs[c * wide + rows : (c + 1) * wide, :] = -re

    def a_src(k, j):
        return send_a.at[pl.ds(pl.multiple_of(j * rows, rows), rows), pl.ds(k * wide, wide)]

    def a_dst(k, j):
        return recv_a.at[k, :, pl.ds(pl.multiple_of(partner_slot(j) * wide, wide), wide)]

    def a_remote(k, j):
        return pltpu.make_async_remote_copy(
            src_ref=a_src(k, j), dst_ref=a_dst(k, j), send_sem=a_send, recv_sem=a_recv.at[k, partner_slot(j) // 4],
            device_id=(slot_strip(j), me_c), device_id_type=MESH,
        )

    def a_local(k):
        last = strips - 1
        return pltpu.make_async_copy(a_src(k, last), a_dst(k, last), a_recv.at[k, nblk - 1])

    for i in range(nblk):
        tab_wait(i)
        cos_rows = tb[4 * i : 4 * i + 4, 0].reshape(4 * rows, side)
        sin_rows = tb[4 * i : 4 * i + 4, 1].reshape(4 * rows, side)
        value = lax.dot_general(cos_rows, xc[...], NT, preferred_element_type=F32)
        value = value + lax.dot_general(sin_rows, xs[...], NT, preferred_element_type=F32)
        send_a[4 * i * rows : 4 * (i + 1) * rows, :] = value.astype(BF16)
        if i == 0:
            pl.semaphore_wait(barrier, strips - 1 + chans - 1)

        @pl.loop(4 * i, min(4 * i + 4, strips - 1))
        def _(j):
            a_remote(0, j).start()

    a_local(0).start()

    load_model.wait()
    ext_hi[:, rows + 2 * HALO :, :] = jnp.zeros((local, 128 - rows - 2 * HALO, side), BF16)
    ext_lo[:, :HALO, :] = jnp.zeros((local, HALO, side), BF16)
    ext_lo[:, rows + HALO :, :] = jnp.zeros((local, 128 - rows - HALO, side), BF16)
    for c in range(local):
        value = m_v[c]
        top = value.astype(BF16)
        ext_hi[c, HALO : HALO + rows, :] = top
        ext_lo[c, HALO : HALO + rows, :] = (value - top.astype(F32)).astype(BF16)
    halo_copies = [
        pltpu.make_async_remote_copy(
            src_ref=ext_hi.at[:, rows : rows + HALO, :], dst_ref=ext_hi.at[:, 0:HALO, :],
            send_sem=h_send.at[0], recv_sem=h_recv.at[0],
            device_id=(strip_next(1), me_c), device_id_type=MESH,
        ),
        pltpu.make_async_remote_copy(
            src_ref=ext_hi.at[:, HALO : 2 * HALO, :], dst_ref=ext_hi.at[:, rows + HALO : rows + 2 * HALO, :],
            send_sem=h_send.at[1], recv_sem=h_recv.at[1],
            device_id=(strip_next(-1), me_c), device_id_type=MESH,
        ),
    ]
    for cp in halo_copies:
        cp.start()

    for k in range(1, local):

        @pl.loop(0, strips - 1)
        def _(j):
            a_remote(k, j).start()

        a_local(k).start()

    row = lax.broadcasted_iota(jnp.int32, (rows, 128), 0)
    col = lax.broadcasted_iota(jnp.int32, (rows, 128), 1)
    shift = col - row - HALO
    total = strips * rows
    base_row = me_s * rows
    band = jnp.zeros((rows, 128), F32)
    for j in range(levels):
        dil = 2**j
        for k in range(filt):
            inner = jnp.zeros((rows, 128), F32)
            for q in range(filt):
                inner = inner + jnp.where(shift == (q - k) * dil, taps[j, q], 0.0)
            detail_row = base_row + row - (k - filt // 2) * dil
            ok = jnp.logical_and(detail_row >= 0, detail_row < total)
            band = band + jnp.where(ok, taps[j, k] * inner, 0.0)
    image_row = base_row + col - HALO
    band = jnp.where(jnp.logical_and(image_row >= 0, image_row < total), band, 0.0)
    band_hi = band.astype(BF16)
    band_lo = (band - band_hi.astype(F32)).astype(BF16)
    x[...] = jnp.zeros(x.shape, BF16)
    for cp in halo_copies:
        cp.wait_recv()
    for c in range(local):
        near = ext_hi[c]
        wav = jnp.dot(band_hi, near, preferred_element_type=F32)
        wav = wav + jnp.dot(band_hi, ext_lo[c], preferred_element_type=F32)
        wav = wav + jnp.dot(band_lo, near, preferred_element_type=F32)
        base[c] = m_v[c] - step[c] * wav

    def b_src(k, peer):
        return send_b.at[
            k, pl.ds(pl.multiple_of(lax.rem(peer, 2) * half, half), half), pl.ds(pl.multiple_of(peer // 2 * 128, 128), 128)
        ]

    def b_remote(k, j):
        peer = chan_peer(j)
        return pltpu.make_async_remote_copy(
            src_ref=b_src(k, peer), dst_ref=recv_b.at[k, me_c], send_sem=b_send, recv_sem=b_recv.at[k],
            device_id=(me_s, peer), device_id_type=MESH,
        )

    def arrive_a(k):
        for g in range(nblk):
            span = 4 * wide
            part = recv_a.at[k, :, g * span : (g + 1) * span]
            pltpu.make_async_copy(part, part, a_recv.at[k, g]).wait()
            dirty = jnp.dot(
                recv_a[k, :, g * span : (g + 1) * span], tb[4 * g : 4 * g + 4].reshape(span, side),
                preferred_element_type=F32,
            )
            value = base[k] + step[k] * dirty
            base[k] = value
            if g == nblk - 1:
                send_b[k] = value.astype(BF16)

        @pl.loop(0, chans - 1)
        def _(j):
            b_remote(k, j).start()

        pltpu.make_async_copy(b_src(k, me_c), recv_b.at[k, me_c], b_recv.at[k]).start()

    def g_remote(k, j):
        return pltpu.make_async_remote_copy(
            src_ref=grecv.at[k, me_c], dst_ref=grecv.at[k, me_c], send_sem=g_send, recv_sem=g_recv.at[k],
            device_id=(me_s, chan_peer(j)), device_id_type=MESH,
        )

    def arrive_b(k):
        part = recv_b.at[k]
        pltpu.make_async_copy(part, part, b_recv.at[k]).wait()
        stage[: chans * half, :] = recv_b[k].astype(F32).reshape(chans * half, 128)
        for m in range(half):
            x[k * chans : (k + 1) * chans, m * 128 : (m + 1) * 128] = stage[pl.ds(m, chans, stride=half), :].astype(BF16)
        part = lax.dot_general(x[k * chans : (k + 1) * chans, :], x[...], NT, preferred_element_type=F32)
        grecv[k, me_c] = part

        @pl.loop(0, chans - 1)
        def _(j):
            g_remote(k, j).start()

    for k in range(local):
        arrive_a(k)
        if k:
            arrive_b(k - 1)
    arrive_b(local - 1)

    size = local * chans
    blocks = []
    for k in range(local):
        part = grecv.at[k, : chans - 1]
        pltpu.make_async_copy(part, part, g_recv.at[k]).wait()
        blocks.append(jnp.sum(grecv[k], axis=0))
    low = jnp.concatenate(blocks, axis=0)[:, :size]
    gi = lax.broadcasted_iota(jnp.int32, (size, size), 0)
    gj = lax.broadcasted_iota(jnp.int32, (size, size), 1)
    identity = jnp.where(gi == gj, 1.0, 0.0).astype(F32)
    strict = jnp.where(gi // chans > gj // chans, low, 0.0)
    upper = lax.dot_general(
        strict, identity, (((0,), (0,)), ((), ())), precision=lax.Precision.HIGHEST, preferred_element_type=F32
    )
    gram = low + upper
    square = jnp.sum(jnp.sum(gram * gram, axis=1, keepdims=True), axis=0, keepdims=True)
    frob = jnp.sqrt(square)
    current = gram / frob
    inverse = 0.5 * (3.0 * identity - current)
    current = exact_dot(current, inverse)
    for it in range(1, NS_ITERS):
        middle = 0.5 * (3.0 * identity - exact_dot(inverse, current))
        if it + 1 < NS_ITERS:
            current = exact_dot(current, middle)
        inverse = exact_dot(middle, inverse)
    factor = shrink[0] * jnp.sqrt(float(rows * side) / frob)
    mix = lax.dot_general(
        inverse, identity, (((0,), (0,)), ((), ())), precision=lax.Precision.HIGHEST, preferred_element_type=F32
    )
    mix = (factor * mix).astype(BF16)

    for q in range(half // 4):
        value = jnp.dot(mix, x[:size, q * 512 : (q + 1) * 512], preferred_element_type=F32)
        for t in range(4):
            stage[pl.ds(q * 4 + t, size, stride=half), :] = value[:, t * 128 : (t + 1) * 128]
    for k in range(local):
        span = chans * half
        send_c[:, k] = stage[k * span : (k + 1) * span, :].reshape(chans, half, 128).astype(BF16)

    mine = polar.at[:, pl.ds(pl.multiple_of(rh * half, half), half), pl.ds(pl.multiple_of(lb * 128, 128), 128)]

    @pl.loop(0, chans - 1)
    def _(j):
        peer = chan_peer(j)
        pltpu.make_async_remote_copy(
            src_ref=send_c.at[peer], dst_ref=mine, send_sem=c_send, recv_sem=c_recv,
            device_id=(me_s, peer), device_id_type=MESH,
        ).start()

    pltpu.make_async_copy(send_c.at[me_c], mine, c_recv).start()
    pltpu.make_async_copy(polar, polar, c_recv).wait()
    for c in range(local):
        out[c] = base[c] - polar[c].astype(F32)

    for cp in halo_copies:
        cp.wait_send()
    for ref, sem in (
        (send_a.at[: (strips - 1) * rows], a_send),
        (recv_b.at[:, : chans - 1], b_send),
        (grecv.at[:, : chans - 1], g_send),
        (send_c.at[: chans - 1], c_send),
    ):
        pltpu.make_async_copy(ref, ref, sem).wait()


def solution(mesh):
    strips, chans = mesh.shape["strip"], mesh.shape["chan"]

    def step_fn(grid, model, step, taps, shrink):
        local, rows, side = model.shape
        wide = 2 * rows
        half = rows // 2
        tab = make_tables(side, strips)
        dma = pltpu.SemaphoreType.DMA
        anywhere = pl.BlockSpec(memory_space=pl.ANY)
        scalars = pl.BlockSpec(memory_space=pltpu.SMEM)
        return pl.pallas_call(
            functools.partial(kernel, strips, chans),
            out_shape=jax.ShapeDtypeStruct((local, rows, side), F32),
            in_specs=[anywhere, anywhere, anywhere, scalars, scalars, scalars],
            out_specs=pl.BlockSpec(memory_space=pltpu.VMEM),
            scratch_shapes=[
                pltpu.VMEM((strips, 2, rows, side), BF16),
                pltpu.VMEM((2, local, rows, side), BF16),
                pltpu.VMEM((local, rows, side), F32),
                pltpu.VMEM((local * wide, side), BF16),
                pltpu.VMEM((local * wide, side), BF16),
                pltpu.VMEM((side, local * wide), BF16),
                pltpu.VMEM((local, rows, strips * wide), BF16),
                pltpu.VMEM((local, 128, side), BF16),
                pltpu.VMEM((local, 128, side), BF16),
                pltpu.VMEM((local, rows, side), F32),
                pltpu.VMEM((local, rows, side), BF16),
                pltpu.VMEM((local, chans, half, 128), BF16),
                pltpu.VMEM((128, half * 128), BF16),
                pltpu.VMEM((local, chans, chans, 128), F32),
                pltpu.VMEM((local * chans * half, 128), F32),
                pltpu.VMEM((chans, local, half, 128), BF16),
                pltpu.VMEM((local, rows, side), BF16),
                dma((2,)), dma((strips // 4,)),
                dma, dma((local, strips // 4)),
                dma, dma((local,)),
                dma, dma((local,)),
                dma, dma,
                dma((2,)), dma((2,)),
            ],
            compiler_params=pltpu.CompilerParams(
                collective_id=0, has_side_effects=True, vmem_limit_bytes=62 * 1024 * 1024
            ),
            name="imaging_step",
        )(tab, grid, model, step, taps, shrink)

    return jax.shard_map(
        step_fn,
        mesh=mesh,
        in_specs=(
            P(None, "chan", "strip", None),
            P("chan", "strip", None),
            P("chan"),
            P(),
            P("strip"),
        ),
        out_specs=P("chan", "strip", None),
        check_vma=False,
    )
```

```python
import functools

import jax
import jax.numpy as jnp
import numpy as np
from jax import lax
from jax.experimental import pallas as pl
from jax.experimental.pallas import tpu as pltpu
from jax.sharding import PartitionSpec as P

NS_ITERS = 5
MESH = pl.DeviceIdType.MESH
HALO = 16
NT = (((1,), (1,)), ((), ()))
F32 = jnp.float32
BF16 = jnp.bfloat16


def make_tables(side, strips):
    index = np.arange(side, dtype=np.int64)
    phases = (index[:, None] * index[None, :] % side) * (2.0 * np.pi / side)
    scale = float(side) ** -0.5
    both = np.stack((np.cos(phases), np.sin(phases))) * scale
    both = both.reshape(2, strips, side // strips, side).swapaxes(0, 1)
    return jnp.asarray(both.astype(np.float32).astype(BF16))


def split(a):
    high = a.astype(BF16)
    return high, (a - high.astype(F32)).astype(BF16)


def split_dot(a, b):
    out = jnp.dot(a[0], b[1], preferred_element_type=F32) + jnp.dot(a[1], b[0], preferred_element_type=F32)
    return out + jnp.dot(a[0], b[0], preferred_element_type=F32)


def kernel(
    strips, chans, tab, grid, model, step, taps, shrink, moved, polar,
    tb, g_v, m_v, xc, xs, send_a, recv_a, ext_hi, ext_lo, base, send_b, recv_b, x, grecv,
    stage, send_c,
    load_sem, tab_sem, a_send, a_recv, b_send, b_recv, g_send, g_recv, c_send, c_recv, h_send, h_recv, out_sem,
):
    me_s = lax.axis_index("strip")
    me_c = lax.axis_index("chan")
    local, rows, side = base.shape
    wide = 2 * rows
    half = rows // 2
    lb = me_c // 2
    rh = lax.rem(me_c, 2)
    levels, filt = taps.shape
    ring = strips // 2
    xring = chans // 4

    z_of = [lax.rem(me_s // 2 + d, ring) * 2 for d in range(ring)]
    z_bit = [lax.rem(me_s, 2), 1 - lax.rem(me_s, 2)]
    steps = [(ring // 2 + ((q + 1) // 2) * (1 - 2 * (q % 2))) % ring for q in range(ring)]
    slots = [(-steps[j // 2] % ring, 1 - j % 2) for j in range(strips)]
    strip_of = [z_of[d] + z_bit[t] for d, t in slots]
    partner = [slots.index((-d % ring, t)) for d, t in slots]

    x_of = [lax.rem(me_c // 2 + d, xring) * 2 for d in range(xring)]
    c_bit = [lax.rem(me_c, 2), 1 - lax.rem(me_c, 2)]
    me_pair = me_c // (2 * xring)
    p_bit = [me_pair * (2 * xring), (1 - me_pair) * (2 * xring)]
    xsteps = [(xring // 2 + ((q + 1) // 2) * (1 - 2 * (q % 2))) % xring for q in range(xring)]
    peers = [p_bit[1 - j // 2 % 2] + x_of[xsteps[j // 4]] + c_bit[1 - j % 2] for j in range(chans - 1)]

    def strip_next(d):
        return lax.rem(me_s + d + strips, strips)

    barrier = pltpu.get_barrier_semaphore()

    for j in range(strips - 1):
        pl.semaphore_signal(barrier, inc=1, device_id=(strip_of[j], me_c), device_id_type=MESH)

    load_grid = pltpu.make_async_copy(grid, g_v, load_sem.at[0])
    load_grid.start()

    def tab_start(i):
        for j in range(4 * i, 4 * i + 4):
            pltpu.make_async_copy(tab.at[strip_of[j]], tb.at[j], tab_sem.at[i]).start()

    def tab_wait(i):
        part = tb.at[4 * i : 4 * i + 4]
        pltpu.make_async_copy(part, part, tab_sem.at[i]).wait()

    tab_start(0)

    for peer in peers:
        pl.semaphore_signal(barrier, inc=1, device_id=(me_s, peer), device_id_type=MESH)

    nblk = strips // 4
    for i in range(1, nblk):
        tab_start(i)
    load_model = pltpu.make_async_copy(model, m_v, load_sem.at[1])
    load_model.start()

    load_grid.wait()
    for c in range(local):
        re = g_v[0, c]
        im = -g_v[1, c]
        xc[c * wide : c * wide + rows, :] = re
        xc[c * wide + rows : (c + 1) * wide, :] = im
        xs[c * wide : c * wide + rows, :] = im
        xs[c * wide + rows : (c + 1) * wide, :] = -re

    def a_src(k, j):
        return send_a.at[j * rows : (j + 1) * rows, k * wide : (k + 1) * wide]

    def a_dst(k, j):
        return recv_a.at[k, :, partner[j] * wide : (partner[j] + 1) * wide]

    def a_remote(k, j):
        return pltpu.make_async_remote_copy(
            src_ref=a_src(k, j), dst_ref=a_dst(k, j), send_sem=a_send, recv_sem=a_recv.at[k, partner[j] // 4],
            device_id=(strip_of[j], me_c), device_id_type=MESH,
        )

    def a_local(k):
        last = strips - 1
        return pltpu.make_async_copy(a_src(k, last), a_dst(k, last), a_recv.at[k, nblk - 1])

    for i in range(nblk):
        tab_wait(i)
        cos_rows = tb[4 * i : 4 * i + 4, 0].reshape(4 * rows, side)
        sin_rows = tb[4 * i : 4 * i + 4, 1].reshape(4 * rows, side)
        value = lax.dot_general(cos_rows, xc[...], NT, preferred_element_type=F32)
        value = value + lax.dot_general(sin_rows, xs[...], NT, preferred_element_type=F32)
        send_a[4 * i * rows : 4 * (i + 1) * rows, :] = value.astype(BF16)
        if i == 0:
            pl.semaphore_wait(barrier, strips - 1 + chans - 1)

        for j in range(4 * i, min(4 * i + 4, strips - 1)):
            a_remote(0, j).start()

    a_local(0).start()

    load_model.wait()
    ext_hi[:, rows + 2 * HALO :, :] = jnp.zeros((local, 128 - rows - 2 * HALO, side), BF16)
    ext_lo[:, :HALO, :] = jnp.zeros((local, HALO, side), BF16)
    ext_lo[:, rows + HALO :, :] = jnp.zeros((local, 128 - rows - HALO, side), BF16)
    for c in range(local):
        value = m_v[c]
        top = value.astype(BF16)
        ext_hi[c, HALO : HALO + rows, :] = top
        ext_lo[c, HALO : HALO + rows, :] = (value - top.astype(F32)).astype(BF16)
    halo_copies = [
        pltpu.make_async_remote_copy(
            src_ref=ext_hi.at[:, rows : rows + HALO, :], dst_ref=ext_hi.at[:, 0:HALO, :],
            send_sem=h_send.at[0], recv_sem=h_recv.at[0],
            device_id=(strip_next(1), me_c), device_id_type=MESH,
        ),
        pltpu.make_async_remote_copy(
            src_ref=ext_hi.at[:, HALO : 2 * HALO, :], dst_ref=ext_hi.at[:, rows + HALO : rows + 2 * HALO, :],
            send_sem=h_send.at[1], recv_sem=h_recv.at[1],
            device_id=(strip_next(-1), me_c), device_id_type=MESH,
        ),
    ]
    for cp in halo_copies:
        cp.start()

    for k in range(1, local):
        for j in range(strips - 1):
            a_remote(k, j).start()

        a_local(k).start()

    row = lax.broadcasted_iota(jnp.int32, (rows, 128), 0)
    col = lax.broadcasted_iota(jnp.int32, (rows, 128), 1)
    shift = col - row - HALO
    total = strips * rows
    base_row = me_s * rows
    band = jnp.zeros((rows, 128), F32)
    for j in range(levels):
        dil = 2**j
        for k in range(filt):
            inner = jnp.zeros((rows, 128), F32)
            for q in range(filt):
                inner = inner + jnp.where(shift == (q - k) * dil, taps[j, q], 0.0)
            detail_row = base_row + row - (k - filt // 2) * dil
            ok = jnp.logical_and(detail_row >= 0, detail_row < total)
            band = band + jnp.where(ok, taps[j, k] * inner, 0.0)
    image_row = base_row + col - HALO
    band = jnp.where(jnp.logical_and(image_row >= 0, image_row < total), band, 0.0)
    band_hi = band.astype(BF16)
    band_lo = (band - band_hi.astype(F32)).astype(BF16)
    x[...] = jnp.zeros(x.shape, BF16)
    def b_src(k, peer):
        return send_b.at[
            k, pl.ds(pl.multiple_of(lax.rem(peer, 2) * half, half), half), pl.ds(pl.multiple_of(peer // 2 * 128, 128), 128)
        ]

    def b_remote(k, peer):
        return pltpu.make_async_remote_copy(
            src_ref=b_src(k, peer), dst_ref=recv_b.at[k, me_c], send_sem=b_send, recv_sem=b_recv.at[k],
            device_id=(me_s, peer), device_id_type=MESH,
        )

    def wavelet():
        for cp in halo_copies:
            cp.wait_recv()
        for c in range(local):
            near = ext_hi[c]
            wav = jnp.dot(band_hi, near, preferred_element_type=F32)
            wav = wav + jnp.dot(band_hi, ext_lo[c], preferred_element_type=F32)
            wav = wav + jnp.dot(band_lo, near, preferred_element_type=F32)
            m_v[c] = m_v[c] - step[c] * wav

    def arrive_a(k):
        for g in range(nblk):
            span = 4 * wide
            part = recv_a.at[k, :, g * span : (g + 1) * span]
            pltpu.make_async_copy(part, part, a_recv.at[k, g]).wait()
            dirty = jnp.dot(
                recv_a[k, :, g * span : (g + 1) * span], tb[4 * g : 4 * g + 4].reshape(span, side),
                preferred_element_type=F32,
            )
            base[k] = base[k] + dirty if g else dirty

    def depart_b(k):
        value = m_v[k] + step[k] * base[k]
        base[k] = value
        send_b[k] = value.astype(BF16)

        for peer in peers:
            b_remote(k, peer).start()

        pltpu.make_async_copy(b_src(k, me_c), recv_b.at[k, me_c], b_recv.at[k]).start()
        pltpu.make_async_copy(base.at[k], moved.at[k], out_sem).start()

    def g_remote(k, peer):
        return pltpu.make_async_remote_copy(
            src_ref=grecv.at[k, me_c], dst_ref=grecv.at[k, me_c], send_sem=g_send, recv_sem=g_recv.at[k],
            device_id=(me_s, peer), device_id_type=MESH,
        )

    def arrive_b(k):
        part = recv_b.at[k]
        pltpu.make_async_copy(part, part, b_recv.at[k]).wait()
        stage[: chans * half, :] = recv_b[k].astype(F32).reshape(chans * half, 128)
        for m in range(half):
            x[k * chans : (k + 1) * chans, m * 128 : (m + 1) * 128] = stage[pl.ds(m, chans, stride=half), :].astype(BF16)
        part = lax.dot_general(x[k * chans : (k + 1) * chans, :], x[...], NT, preferred_element_type=F32)
        grecv[k, me_c] = part[: chans // 2] + pltpu.roll(part[chans // 2 :], size, 1)

        for peer in peers:
            g_remote(k, peer).start()

    last = local - 1
    size = local * chans
    for k in range(last):
        arrive_a(k)
        if k == 1:
            wavelet()
            depart_b(0)
        if k:
            depart_b(k)
    for k in range(last - 1):
        arrive_b(k)
    arrive_a(last)
    depart_b(last)
    arrive_b(last - 1)
    arrive_b(last)

    blocks = []
    for k in range(local):
        part = grecv.at[k, : chans - 1]
        pltpu.make_async_copy(part, part, g_recv.at[k]).wait()
        part = jnp.sum(grecv[k], axis=0)
        blocks += [part, pltpu.roll(part, size, 1)]
    low = jnp.concatenate(blocks, axis=0)[:, :size]
    gi = lax.broadcasted_iota(jnp.int32, (size, size), 0)
    gj = lax.broadcasted_iota(jnp.int32, (size, size), 1)
    identity = jnp.where(gi == gj, 1.0, 0.0).astype(F32)
    strict = jnp.where(gi // chans > gj // chans, low, 0.0)
    upper = lax.dot_general(
        strict, identity, (((0,), (0,)), ((), ())), precision=lax.Precision.HIGHEST, preferred_element_type=F32
    )
    gram = low + upper
    square = jnp.sum(jnp.sum(gram * gram, axis=1, keepdims=True), axis=0, keepdims=True)
    frob = jnp.sqrt(square)
    current = gram / frob
    inverse = 0.5 * (3.0 * identity - current)
    current = split_dot(split(current), split(inverse))
    for it in range(1, NS_ITERS):
        parts = split(inverse)
        halves = split(current)
        middle = split(0.5 * (3.0 * identity - split_dot(parts, halves)))
        if it + 1 < NS_ITERS:
            current = split_dot(halves, middle)
        inverse = split_dot(middle, parts)
    mix = (shrink[0] * jnp.sqrt(float(rows * side) / frob) * inverse).astype(BF16)

    quarter = half // 2
    span = chans * quarter
    for h in range(2):
        for q in range(quarter // 4):
            first = (h * quarter + q * 4) * 128
            value = jnp.dot(mix, x[:size, first : first + 512], preferred_element_type=F32)
            for t in range(4):
                stage[pl.ds(q * 4 + t, size, stride=quarter), :] = value[:, t * 128 : (t + 1) * 128]
        for k in range(local):
            send_c[h, :, k] = stage[k * span : (k + 1) * span, :].reshape(chans, quarter, 128).astype(BF16)
        mine = polar.at[
            :, pl.ds(pl.multiple_of(rh * half + h * quarter, quarter), quarter), pl.ds(pl.multiple_of(lb * 128, 128), 128)
        ]

        for peer in peers:
            pltpu.make_async_remote_copy(
                src_ref=send_c.at[h, peer], dst_ref=mine, send_sem=c_send, recv_sem=c_recv,
                device_id=(me_s, peer), device_id_type=MESH,
            ).start()

        pltpu.make_async_copy(send_c.at[h, me_c], mine, c_recv).start()
    pltpu.make_async_copy(base, moved, out_sem).wait()
    pltpu.make_async_copy(polar, polar, c_recv).wait()

    for cp in halo_copies:
        cp.wait_send()
    for ref, sem in (
        (send_a.at[: (strips - 1) * rows], a_send),
        (recv_b.at[:, : chans - 1], b_send),
        (grecv.at[:, : chans - 1], g_send),
        (send_c.at[:, : chans - 1], c_send),
    ):
        pltpu.make_async_copy(ref, ref, sem).wait()


def solution(mesh):
    strips, chans = mesh.shape["strip"], mesh.shape["chan"]

    def step_fn(grid, model, step, taps, shrink):
        local, rows, side = model.shape
        wide = 2 * rows
        half = rows // 2
        tab = make_tables(side, strips)
        dma = pltpu.SemaphoreType.DMA
        anywhere = pl.BlockSpec(memory_space=pl.ANY)
        scalars = pl.BlockSpec(memory_space=pltpu.SMEM)
        moved, polar = pl.pallas_call(
            functools.partial(kernel, strips, chans),
            out_shape=(
                pltpu.VMEM((local, rows, side), F32),
                pltpu.VMEM((local, rows, side), BF16),
            ),
            in_specs=[anywhere, anywhere, anywhere, scalars, scalars, scalars],
            out_specs=(pl.BlockSpec(memory_space=pltpu.VMEM),) * 2,
            scratch_shapes=[
                pltpu.VMEM((strips, 2, rows, side), BF16),
                pltpu.VMEM((2, local, rows, side), BF16),
                pltpu.VMEM((local, rows, side), F32),
                pltpu.VMEM((local * wide, side), BF16),
                pltpu.VMEM((local * wide, side), BF16),
                pltpu.VMEM((side, local * wide), BF16),
                pltpu.VMEM((local, rows, strips * wide), BF16),
                pltpu.VMEM((local, 128, side), BF16),
                pltpu.VMEM((local, 128, side), BF16),
                pltpu.VMEM((local, rows, side), F32),
                pltpu.VMEM((local, rows, side), BF16),
                pltpu.VMEM((local, chans, half, 128), BF16),
                pltpu.VMEM((128, half * 128), BF16),
                pltpu.VMEM((local, chans, chans // 2, 128), F32),
                pltpu.VMEM((local * chans * half // 2, 128), F32),
                pltpu.VMEM((2, chans, local, half // 2, 128), BF16),
                dma((2,)), dma((strips // 4,)),
                dma, dma((local, strips // 4)),
                dma, dma((local,)),
                dma, dma((local,)),
                dma, dma,
                dma((2,)), dma((2,)), dma,
            ],
            compiler_params=pltpu.CompilerParams(
                collective_id=0, has_side_effects=True, vmem_limit_bytes=60 * 1024 * 1024
            ),
            name="imaging_step",
        )(tab, grid, model, step, taps, shrink)
        return moved - polar.astype(F32)

    return jax.shard_map(
        step_fn,
        mesh=mesh,
        in_specs=(
            P(None, "chan", "strip", None),
            P("chan", "strip", None),
            P("chan"),
            P(),
            P("strip"),
        ),
        out_specs=P("chan", "strip", None),
        check_vma=False,
    )
```

```python
import functools

import jax
import jax.numpy as jnp
import numpy as np
from jax import lax
from jax.experimental import pallas as pl
from jax.experimental.pallas import tpu as pltpu
from jax.sharding import PartitionSpec as P

NS_ITERS = 5
MESH = pl.DeviceIdType.MESH
NT = (((1,), (1,)), ((), ()))
F32 = jnp.float32
BF16 = jnp.bfloat16


def make_tables(side, strips):
    index = np.arange(side, dtype=np.int64)
    phases = (index[:, None] * index[None, :] % side) * (2.0 * np.pi / side)
    scale = float(side) ** -0.5
    both = np.stack((np.cos(phases), np.sin(phases))) * scale
    both = both.reshape(2, strips, side // strips, side).swapaxes(0, 1)
    return jnp.asarray(both.astype(np.float32).astype(BF16))


def split(a):
    high = a.astype(BF16)
    return high, (a - high.astype(F32)).astype(BF16)


def split_dot(a, b):
    out = jnp.dot(a[0], b[1], preferred_element_type=F32) + jnp.dot(a[1], b[0], preferred_element_type=F32)
    return out + jnp.dot(a[0], b[0], preferred_element_type=F32)


def kernel(
    strips, chans, tab, grid, model, step, taps, shrink, moved, polar,
    tb, g_v, m_v, xc, xs, send_a, recv_a, own_hi, own_lo, base, send_b, recv_b, x, grecv,
    stage, send_c, relay, edge, halo_out, halo_in, bands,
    load_sem, tab_sem, a_send, a_recv, b_send, b_recv, g_send, g_recv, c_send, c_recv, h_send, h_recv, out_sem,
):
    me_s = lax.axis_index("strip")
    me_c = lax.axis_index("chan")
    local, rows, side = base.shape
    wide = 2 * rows
    half = rows // 2
    lb = me_c // 2
    rh = lax.rem(me_c, 2)
    levels, filt = taps.shape
    reach = (filt - 1) * 2 ** (levels - 1)
    ring = strips // 2
    xring = chans // 4

    z_of = [lax.rem(me_s // 2 + d, ring) * 2 for d in range(ring)]
    z_bit = [lax.rem(me_s, 2), 1 - lax.rem(me_s, 2)]
    steps = [(ring // 2 + ((q + 1) // 2) * (1 - 2 * (q % 2))) % ring for q in range(ring)]
    slots = [(-steps[j // 2] % ring, 1 - j % 2) for j in range(strips)]
    strip_of = [z_of[d] + z_bit[t] for d, t in slots]
    partner = [slots.index((-d % ring, t)) for d, t in slots]

    x_of = [lax.rem(me_c // 2 + d, xring) * 2 for d in range(xring)]
    c_bit = [lax.rem(me_c, 2), 1 - lax.rem(me_c, 2)]
    me_pair = me_c // (2 * xring)
    p_bit = [me_pair * (2 * xring), (1 - me_pair) * (2 * xring)]
    xsteps = [(xring // 2 + ((q + 1) // 2) * (1 - 2 * (q % 2))) % xring for q in range(xring)]
    peers = [p_bit[1 - j // 2 % 2] + x_of[xsteps[j // 4]] + c_bit[1 - j % 2] for j in range(chans - 1)]

    def strip_next(d):
        return lax.rem(me_s + d + strips, strips)

    barrier = pltpu.get_barrier_semaphore()

    for j in range(strips - 1):
        pl.semaphore_signal(barrier, inc=1, device_id=(strip_of[j], me_c), device_id_type=MESH)

    load_grid = pltpu.make_async_copy(grid, g_v, load_sem.at[0])
    load_grid.start()

    def tab_start(i):
        for j in range(4 * i, 4 * i + 4):
            pltpu.make_async_copy(tab.at[strip_of[j]], tb.at[j], tab_sem.at[i]).start()

    def tab_wait(i):
        part = tb.at[4 * i : 4 * i + 4]
        pltpu.make_async_copy(part, part, tab_sem.at[i]).wait()

    tab_start(0)

    for peer in peers:
        pl.semaphore_signal(barrier, inc=1, device_id=(me_s, peer), device_id_type=MESH)

    nblk = strips // 4
    for i in range(1, nblk):
        tab_start(i)
    load_model = pltpu.make_async_copy(model, m_v, load_sem.at[1])
    load_model.start()

    load_grid.wait()
    for c in range(local):
        re = g_v[0, c]
        im = -g_v[1, c]
        xc[c * wide : c * wide + rows, :] = re
        xc[c * wide + rows : (c + 1) * wide, :] = im
        xs[c * wide : c * wide + rows, :] = im
        xs[c * wide + rows : (c + 1) * wide, :] = -re

    pieces = [(k, 0, rows) for k in range(local - 1)] + [(local - 1, 0, half), (local - 1, half, rows)]

    def a_src(p, j):
        k, top, end = pieces[p]
        return send_a.at[j * rows + top : j * rows + end, k * wide : (k + 1) * wide]

    def a_dst(p, j):
        k, top, end = pieces[p]
        return recv_a.at[k, top:end, partner[j] * wide : (partner[j] + 1) * wide]

    def a_remote(k, j):
        return pltpu.make_async_remote_copy(
            src_ref=a_src(k, j), dst_ref=a_dst(k, j), send_sem=a_send, recv_sem=a_recv.at[k, partner[j] // 4],
            device_id=(strip_of[j], me_c), device_id_type=MESH,
        )

    def a_local(k):
        last = strips - 1
        return pltpu.make_async_copy(a_src(k, last), a_dst(k, last), a_recv.at[k, nblk - 1])

    load_model.wait()
    for c in range(local):
        value = m_v[c]
        top = value.astype(BF16)
        own_hi[c] = top
        own_lo[c] = (value - top.astype(F32)).astype(BF16)
        edge[0, c * reach : (c + 1) * reach] = m_v[c, rows - reach :]
        edge[1, c * reach : (c + 1) * reach] = m_v[c, :reach]
    halo_out[...] = edge[...].astype(BF16)
    bit = lax.rem(me_s, 2)
    part = side // 2
    pair = 1 - 2 * bit

    def leg(i, src, dst, to):
        return pltpu.make_async_remote_copy(
            src_ref=src, dst_ref=dst, send_sem=h_send.at[i], recv_sem=h_recv.at[i],
            device_id=(strip_next(to), me_c), device_id_type=MESH,
        )

    legs = [
        leg(0, halo_out.at[bit], halo_in.at[bit], pair),
        leg(1, halo_out.at[1 - bit, :, :part], halo_in.at[1 - bit, :, :part], -pair),
        leg(2, halo_out.at[1 - bit, :, part:], relay, pair),
    ]

    for i in range(nblk):
        tab_wait(i)
        cos_rows = tb[4 * i : 4 * i + 4, 0].reshape(4 * rows, side)
        sin_rows = tb[4 * i : 4 * i + 4, 1].reshape(4 * rows, side)
        value = lax.dot_general(cos_rows, xc[...], NT, preferred_element_type=F32)
        value = value + lax.dot_general(sin_rows, xs[...], NT, preferred_element_type=F32)
        send_a[4 * i * rows : 4 * (i + 1) * rows, :] = value.astype(BF16)
        if i == 0:
            pl.semaphore_wait(barrier, strips - 1 + chans - 1)
            for i_leg in (2, 0, 1):
                legs[i_leg].start()

        for j in range(4 * i, min(4 * i + 4, strips - 1)):
            a_remote(0, j).start()

    a_local(0).start()

    for j in range(strips - 1):
        a_remote(1, j).start()
    a_local(1).start()
    legs[2].wait_recv()
    leg(3, relay, halo_in.at[bit, :, part:], 2 * pair).start()
    for k in range(2, local + 1):
        for j in range(strips - 1):
            a_remote(k, j).start()
        a_local(k).start()

    total = strips * rows
    base_row = me_s * rows
    row = lax.broadcasted_iota(jnp.int32, (rows, 256), 0)
    col = lax.broadcasted_iota(jnp.int32, (rows, 256), 1)
    for c in range(local):
        before = col - rows - c * reach
        after = before - local * reach
        own = col < rows
        in_before = jnp.logical_and(before >= 0, before < reach)
        in_after = jnp.logical_and(after >= 0, after < reach)
        place = jnp.where(own, col, jnp.where(in_before, before - reach, rows + after))
        shift = place - row
        band = jnp.zeros((rows, 256), F32)
        for j in range(levels):
            dil = 2**j
            for k in range(filt):
                inner = jnp.zeros((rows, 256), F32)
                for q in range(filt):
                    inner = inner + jnp.where(shift == (q - k) * dil, taps[j, q], 0.0)
                detail_row = base_row + row - (k - filt // 2) * dil
                ok = jnp.logical_and(detail_row >= 0, detail_row < total)
                band = band + jnp.where(ok, taps[j, k] * inner, 0.0)
        image_row = base_row + place
        known = jnp.logical_or(own, jnp.logical_or(in_before, in_after))
        known = jnp.logical_and(known, jnp.logical_and(image_row >= 0, image_row < total))
        band = jnp.where(known, band, 0.0)
        band_hi = band.astype(BF16)
        bands[c, 0] = band_hi
        bands[c, 1] = (band - band_hi.astype(F32)).astype(BF16)
    x[...] = jnp.zeros(x.shape, BF16)
    def b_src(k, peer):
        return send_b.at[
            k, pl.ds(pl.multiple_of(lax.rem(peer, 2) * half, half), half), pl.ds(pl.multiple_of(peer // 2 * 128, 128), 128)
        ]

    def b_remote(k, peer):
        return pltpu.make_async_remote_copy(
            src_ref=b_src(k, peer), dst_ref=recv_b.at[k, me_c], send_sem=b_send, recv_sem=b_recv.at[k],
            device_id=(me_s, peer), device_id_type=MESH,
        )

    def wavelet():
        for ref, i in ((halo_in.at[0], 0), (relay, 1), (relay, 3)):
            pltpu.make_async_copy(ref, ref, h_recv.at[i]).wait()
        filler = jnp.zeros((256 - rows - 2 * local * reach, side), BF16)
        for c in range(local):
            near = jnp.concatenate((own_hi[c], halo_in[0], halo_in[1], filler), axis=0)
            wav = jnp.dot(bands[c, 0], near, preferred_element_type=F32)
            wav = wav + jnp.dot(bands[c, 0, :, :rows], own_lo[c], preferred_element_type=F32)
            wav = wav + jnp.dot(bands[c, 1], near, preferred_element_type=F32)
            m_v[c] = m_v[c] - step[c] * wav

    def arrive_a(p):
        k, top, end = pieces[p]
        for g in range(nblk):
            span = 4 * wide
            part = recv_a.at[k, top:end, g * span : (g + 1) * span]
            pltpu.make_async_copy(part, part, a_recv.at[p, g]).wait()
            dirty = jnp.dot(
                recv_a[k, top:end, g * span : (g + 1) * span], tb[4 * g : 4 * g + 4].reshape(span, side),
                preferred_element_type=F32,
            )
            base[k, top:end] = base[k, top:end] + dirty if g else dirty

    def depart_b(p):
        k, top, end = pieces[p]
        value = m_v[k, top:end] + step[k] * base[k, top:end]
        base[k, top:end] = value
        send_b[k, top:end] = value.astype(BF16)
        pltpu.make_async_copy(base.at[k, top:end], moved.at[k, top:end], out_sem).start()
        if end - top == rows:
            for peer in peers:
                b_remote(k, peer).start()
            pltpu.make_async_copy(b_src(k, me_c), recv_b.at[k, me_c], b_recv.at[k]).start()
            return
        core = top // half
        for j in range(0, chans - 2, 2):
            b_remote(k, p_bit[1 - j // 2 % 2] + x_of[xsteps[j // 4]] + core).start()

        @pl.when(rh == core)
        def _():
            pltpu.make_async_copy(b_src(k, me_c), recv_b.at[k, me_c], b_recv.at[k]).start()

        @pl.when(rh != core)
        def _():
            b_remote(k, peers[-1]).start()

    def g_remote(k, peer):
        return pltpu.make_async_remote_copy(
            src_ref=grecv.at[k, me_c], dst_ref=grecv.at[k, me_c], send_sem=g_send, recv_sem=g_recv.at[k],
            device_id=(me_s, peer), device_id_type=MESH,
        )

    def arrive_b(k):
        part = recv_b.at[k]
        pltpu.make_async_copy(part, part, b_recv.at[k]).wait()
        stage[: chans * half, :] = recv_b[k].astype(F32).reshape(chans * half, 128)
        for m in range(half):
            x[k * chans : (k + 1) * chans, m * 128 : (m + 1) * 128] = stage[pl.ds(m, chans, stride=half), :].astype(BF16)
        part = lax.dot_general(x[k * chans : (k + 1) * chans, :], x[...], NT, preferred_element_type=F32)
        grecv[k, me_c] = part[: chans // 2] + pltpu.roll(part[chans // 2 :], size, 1)

        for peer in peers:
            g_remote(k, peer).start()

    last = local - 1
    size = local * chans
    for k in range(last):
        arrive_a(k)
        if k == 1:
            wavelet()
            depart_b(0)
        if k:
            depart_b(k)
    for k in range(last - 1):
        arrive_b(k)
    arrive_a(last)
    depart_b(last)
    arrive_a(last + 1)
    depart_b(last + 1)
    arrive_b(last - 1)
    arrive_b(last)

    blocks = []
    for k in range(local):
        part = grecv.at[k, : chans - 1]
        pltpu.make_async_copy(part, part, g_recv.at[k]).wait()
        part = jnp.sum(grecv[k], axis=0)
        blocks += [part, pltpu.roll(part, size, 1)]
    low = jnp.concatenate(blocks, axis=0)[:, :size]
    gi = lax.broadcasted_iota(jnp.int32, (size, size), 0)
    gj = lax.broadcasted_iota(jnp.int32, (size, size), 1)
    identity = jnp.where(gi == gj, 1.0, 0.0).astype(F32)
    strict = jnp.where(gi // chans > gj // chans, low, 0.0)
    upper = lax.dot_general(
        strict, identity, (((0,), (0,)), ((), ())), precision=lax.Precision.HIGHEST, preferred_element_type=F32
    )
    gram = low + upper
    square = jnp.sum(jnp.sum(gram * gram, axis=1, keepdims=True), axis=0, keepdims=True)
    frob = jnp.sqrt(square)
    current = gram / frob
    inverse = 0.5 * (3.0 * identity - current)
    current = split_dot(split(current), split(inverse))
    for it in range(1, NS_ITERS):
        parts = split(inverse)
        halves = split(current)
        middle = split(0.5 * (3.0 * identity - split_dot(parts, halves)))
        if it + 1 < NS_ITERS:
            current = split_dot(halves, middle)
        inverse = split_dot(middle, parts)
    mix = (shrink[0] * jnp.sqrt(float(rows * side) / frob) * inverse).astype(BF16)

    quarter = half // 2
    span = chans * quarter
    for h in range(2):
        for q in range(quarter // 4):
            first = (h * quarter + q * 4) * 128
            value = jnp.dot(mix, x[:size, first : first + 512], preferred_element_type=F32)
            for t in range(4):
                stage[pl.ds(q * 4 + t, size, stride=quarter), :] = value[:, t * 128 : (t + 1) * 128]
        for k in range(local):
            send_c[h, :, k] = stage[k * span : (k + 1) * span, :].reshape(chans, quarter, 128).astype(BF16)
        mine = polar.at[
            :, pl.ds(pl.multiple_of(rh * half + h * quarter, quarter), quarter), pl.ds(pl.multiple_of(lb * 128, 128), 128)
        ]

        for peer in peers:
            pltpu.make_async_remote_copy(
                src_ref=send_c.at[h, peer], dst_ref=mine, send_sem=c_send, recv_sem=c_recv,
                device_id=(me_s, peer), device_id_type=MESH,
            ).start()

        pltpu.make_async_copy(send_c.at[h, me_c], mine, c_recv).start()
    pltpu.make_async_copy(base, moved, out_sem).wait()
    pltpu.make_async_copy(polar, polar, c_recv).wait()

    for ref, i in ((halo_out.at[0], 0), (relay, 1), (relay, 2), (relay, 3)):
        pltpu.make_async_copy(ref, ref, h_send.at[i]).wait()
    for ref, sem in (
        (send_a.at[: (strips - 1) * rows], a_send),
        (recv_b.at[:, : chans - 1], b_send),
        (grecv.at[:, : chans - 1], g_send),
        (send_c.at[:, : chans - 1], c_send),
    ):
        pltpu.make_async_copy(ref, ref, sem).wait()


def solution(mesh):
    strips, chans = mesh.shape["strip"], mesh.shape["chan"]

    def step_fn(grid, model, step, taps, shrink):
        local, rows, side = model.shape
        wide = 2 * rows
        half = rows // 2
        reach = (taps.shape[1] - 1) * 2 ** (taps.shape[0] - 1)
        tab = make_tables(side, strips)
        dma = pltpu.SemaphoreType.DMA
        anywhere = pl.BlockSpec(memory_space=pl.ANY)
        scalars = pl.BlockSpec(memory_space=pltpu.SMEM)
        moved, polar = pl.pallas_call(
            functools.partial(kernel, strips, chans),
            out_shape=(
                pltpu.VMEM((local, rows, side), F32),
                pltpu.VMEM((local, rows, side), BF16),
            ),
            in_specs=[anywhere, anywhere, anywhere, scalars, scalars, scalars],
            out_specs=(pl.BlockSpec(memory_space=pltpu.VMEM),) * 2,
            scratch_shapes=[
                pltpu.VMEM((strips, 2, rows, side), BF16),
                pltpu.VMEM((2, local, rows, side), BF16),
                pltpu.VMEM((local, rows, side), F32),
                pltpu.VMEM((local * wide, side), BF16),
                pltpu.VMEM((local * wide, side), BF16),
                pltpu.VMEM((side, local * wide), BF16),
                pltpu.VMEM((local, rows, strips * wide), BF16),
                pltpu.VMEM((local, rows, side), BF16),
                pltpu.VMEM((local, rows, side), BF16),
                pltpu.VMEM((local, rows, side), F32),
                pltpu.VMEM((local, rows, side), BF16),
                pltpu.VMEM((local, chans, half, 128), BF16),
                pltpu.VMEM((128, half * 128), BF16),
                pltpu.VMEM((local, chans, chans // 2, 128), F32),
                pltpu.VMEM((local * chans * half // 2, 128), F32),
                pltpu.VMEM((2, chans, local, half // 2, 128), BF16),
                pltpu.VMEM((local * reach, side // 2), BF16),
                pltpu.VMEM((2, local * reach, side), F32),
                pltpu.VMEM((2, local * reach, side), BF16),
                pltpu.VMEM((2, local * reach, side), BF16),
                pltpu.VMEM((local, 2, rows, 256), BF16),
                dma((2,)), dma((strips // 4,)),
                dma, dma((local + 1, strips // 4)),
                dma, dma((local,)),
                dma, dma((local,)),
                dma, dma,
                dma((4,)), dma((4,)), dma,
            ],
            compiler_params=pltpu.CompilerParams(
                collective_id=0, has_side_effects=True, vmem_limit_bytes=60 * 1024 * 1024
            ),
            name="imaging_step",
        )(tab, grid, model, step, taps, shrink)
        return moved - polar.astype(F32)

    return jax.shard_map(
        step_fn,
        mesh=mesh,
        in_specs=(
            P(None, "chan", "strip", None),
            P("chan", "strip", None),
            P("chan"),
            P(),
            P("strip"),
        ),
        out_specs=P("chan", "strip", None),
        check_vma=False,
    )
```

```python
import functools

import jax
import jax.numpy as jnp
import numpy as np
from jax import lax
from jax.experimental import pallas as pl
from jax.experimental.pallas import tpu as pltpu
from jax.sharding import PartitionSpec as P

NS_ITERS = 5
MESH = pl.DeviceIdType.MESH
NT = (((1,), (1,)), ((), ()))
F32 = jnp.float32
BF16 = jnp.bfloat16


def make_tables(side, strips):
    index = np.arange(side, dtype=np.int64)
    phases = (index[:, None] * index[None, :] % side) * (2.0 * np.pi / side)
    scale = float(side) ** -0.5
    both = np.stack((np.cos(phases), np.sin(phases))) * scale
    both = both.reshape(2, strips, side // strips, side).swapaxes(0, 1)
    return jnp.asarray(both.astype(np.float32).astype(BF16))


def split(a):
    high = a.astype(BF16)
    return high, (a - high.astype(F32)).astype(BF16)


def split_dot(a, b):
    out = jnp.dot(a[0], b[1], preferred_element_type=F32) + jnp.dot(a[1], b[0], preferred_element_type=F32)
    return out + jnp.dot(a[0], b[0], preferred_element_type=F32)


def kernel(
    strips, chans, tab, grid, model, step, taps, shrink, moved, polar,
    tb, g_v, m_v, xc, xs, send_a, recv_a, own_hi, own_lo, base, send_b, recv_b, x, grecv,
    stage, send_c, relay, edge, halo_out, halo_in, bands,
    load_sem, tab_sem, a_send, a_recv, b_send, b_recv, g_send, g_recv, c_send, c_recv, h_send, h_recv, out_sem,
):
    me_s = lax.axis_index("strip")
    me_c = lax.axis_index("chan")
    local, rows, side = base.shape
    wide = 2 * rows
    half = rows // 2
    lb = me_c // 2
    rh = lax.rem(me_c, 2)
    levels, filt = taps.shape
    reach = (filt - 1) * 2 ** (levels - 1)
    ring = strips // 2
    xring = chans // 4

    z_of = [lax.rem(me_s // 2 + d, ring) * 2 for d in range(ring)]
    z_bit = [lax.rem(me_s, 2), 1 - lax.rem(me_s, 2)]
    steps = [(ring // 2 + ((q + 1) // 2) * (1 - 2 * (q % 2))) % ring for q in range(ring)]
    slots = [(-steps[j // 2] % ring, 1 - j % 2) for j in range(strips)]
    strip_of = [z_of[d] + z_bit[t] for d, t in slots]
    partner = [slots.index((-d % ring, t)) for d, t in slots]

    x_of = [lax.rem(me_c // 2 + d, xring) * 2 for d in range(xring)]
    c_bit = [lax.rem(me_c, 2), 1 - lax.rem(me_c, 2)]
    me_pair = me_c // (2 * xring)
    p_bit = [me_pair * (2 * xring), (1 - me_pair) * (2 * xring)]
    xsteps = [(xring // 2 + ((q + 1) // 2) * (1 - 2 * (q % 2))) % xring for q in range(xring)]
    peers = [p_bit[1 - j // 2 % 2] + x_of[xsteps[j // 4]] + c_bit[1 - j % 2] for j in range(chans - 1)]

    def strip_next(d):
        return lax.rem(me_s + d + strips, strips)

    barrier = pltpu.get_barrier_semaphore()

    for j in range(strips - 1):
        pl.semaphore_signal(barrier, inc=1, device_id=(strip_of[j], me_c), device_id_type=MESH)

    load_grid = pltpu.make_async_copy(grid, g_v, load_sem.at[0])
    load_grid.start()

    def tab_start(i):
        for j in range(4 * i, 4 * i + 4):
            pltpu.make_async_copy(tab.at[strip_of[j]], tb.at[j], tab_sem.at[i]).start()

    def tab_wait(i):
        part = tb.at[4 * i : 4 * i + 4]
        pltpu.make_async_copy(part, part, tab_sem.at[i]).wait()

    tab_start(0)

    for peer in peers:
        pl.semaphore_signal(barrier, inc=1, device_id=(me_s, peer), device_id_type=MESH)

    nblk = strips // 4
    for i in range(1, nblk):
        tab_start(i)
    load_model = pltpu.make_async_copy(model, m_v, load_sem.at[1])
    load_model.start()

    load_grid.wait()
    for c in range(local):
        re = g_v[0, c]
        im = -g_v[1, c]
        xc[c * wide : c * wide + rows, :] = re
        xc[c * wide + rows : (c + 1) * wide, :] = im
        xs[c * wide : c * wide + rows, :] = im
        xs[c * wide + rows : (c + 1) * wide, :] = -re

    pieces = [(k, 0, rows) for k in range(local - 1)] + [(local - 1, 0, half), (local - 1, half, rows)]

    def a_src(p, j):
        k, top, end = pieces[p]
        return send_a.at[j * rows + top : j * rows + end, k * wide : (k + 1) * wide]

    def a_dst(p, j):
        k, top, end = pieces[p]
        return recv_a.at[k, top:end, partner[j] * wide : (partner[j] + 1) * wide]

    def a_remote(k, j):
        return pltpu.make_async_remote_copy(
            src_ref=a_src(k, j), dst_ref=a_dst(k, j), send_sem=a_send, recv_sem=a_recv.at[k, partner[j] // 4],
            device_id=(strip_of[j], me_c), device_id_type=MESH,
        )

    def a_local(k):
        last = strips - 1
        return pltpu.make_async_copy(a_src(k, last), a_dst(k, last), a_recv.at[k, nblk - 1])

    load_model.wait()
    for c in range(local):
        value = m_v[c]
        top = value.astype(BF16)
        own_hi[c] = top
        own_lo[c] = (value - top.astype(F32)).astype(BF16)
        edge[0, c * reach : (c + 1) * reach] = m_v[c, rows - reach :]
        edge[1, c * reach : (c + 1) * reach] = m_v[c, :reach]
    halo_out[...] = edge[...].astype(BF16)
    bit = lax.rem(me_s, 2)
    part = side // 2
    pair = 1 - 2 * bit

    def leg(i, src, dst, to):
        return pltpu.make_async_remote_copy(
            src_ref=src, dst_ref=dst, send_sem=h_send.at[i], recv_sem=h_recv.at[i],
            device_id=(strip_next(to), me_c), device_id_type=MESH,
        )

    legs = [
        leg(0, halo_out.at[bit], halo_in.at[bit], pair),
        leg(1, halo_out.at[1 - bit, :, :part], halo_in.at[1 - bit, :, :part], -pair),
        leg(2, halo_out.at[1 - bit, :, part:], relay, pair),
    ]

    for i in range(nblk):
        tab_wait(i)
        cos_rows = tb[4 * i : 4 * i + 4, 0].reshape(4 * rows, side)
        sin_rows = tb[4 * i : 4 * i + 4, 1].reshape(4 * rows, side)
        value = lax.dot_general(cos_rows, xc[...], NT, preferred_element_type=F32)
        value = value + lax.dot_general(sin_rows, xs[...], NT, preferred_element_type=F32)
        send_a[4 * i * rows : 4 * (i + 1) * rows, :] = value.astype(BF16)
        if i == 0:
            pl.semaphore_wait(barrier, strips - 1 + chans - 1)
            for i_leg in (2, 0, 1):
                legs[i_leg].start()

        for j in range(4 * i, min(4 * i + 4, strips - 1)):
            a_remote(0, j).start()

    a_local(0).start()

    for j in range(strips - 1):
        a_remote(1, j).start()
    a_local(1).start()
    legs[2].wait_recv()
    leg(3, relay, halo_in.at[bit, :, part:], 2 * pair).start()
    for k in range(2, local + 1):
        for j in range(strips - 1):
            a_remote(k, j).start()
        a_local(k).start()

    total = strips * rows
    base_row = me_s * rows
    row = lax.broadcasted_iota(jnp.int32, (rows, 256), 0)
    col = lax.broadcasted_iota(jnp.int32, (rows, 256), 1)
    for c in range(local):
        before = col - rows - c * reach
        after = before - local * reach
        own = col < rows
        in_before = jnp.logical_and(before >= 0, before < reach)
        in_after = jnp.logical_and(after >= 0, after < reach)
        place = jnp.where(own, col, jnp.where(in_before, before - reach, rows + after))
        shift = place - row
        band = jnp.zeros((rows, 256), F32)
        for j in range(levels):
            dil = 2**j
            for k in range(filt):
                inner = jnp.zeros((rows, 256), F32)
                for q in range(filt):
                    inner = inner + jnp.where(shift == (q - k) * dil, taps[j, q], 0.0)
                detail_row = base_row + row - (k - filt // 2) * dil
                ok = jnp.logical_and(detail_row >= 0, detail_row < total)
                band = band + jnp.where(ok, taps[j, k] * inner, 0.0)
        image_row = base_row + place
        known = jnp.logical_or(own, jnp.logical_or(in_before, in_after))
        known = jnp.logical_and(known, jnp.logical_and(image_row >= 0, image_row < total))
        band = jnp.where(known, band, 0.0)
        band_hi = band.astype(BF16)
        bands[c, 0] = band_hi
        bands[c, 1] = (band - band_hi.astype(F32)).astype(BF16)
    x[...] = jnp.zeros(x.shape, BF16)
    def b_src(k, peer):
        return send_b.at[
            k, pl.ds(pl.multiple_of(lax.rem(peer, 2) * half, half), half), pl.ds(pl.multiple_of(peer // 2 * 128, 128), 128)
        ]

    def b_remote(k, peer):
        return pltpu.make_async_remote_copy(
            src_ref=b_src(k, peer), dst_ref=recv_b.at[k, me_c], send_sem=b_send, recv_sem=b_recv.at[k],
            device_id=(me_s, peer), device_id_type=MESH,
        )

    def wavelet():
        for ref, i in ((halo_in.at[0], 0), (relay, 1), (relay, 3)):
            pltpu.make_async_copy(ref, ref, h_recv.at[i]).wait()
        filler = jnp.zeros((256 - rows - 2 * local * reach, side), BF16)
        for c in range(local):
            near = jnp.concatenate((own_hi[c], halo_in[0], halo_in[1], filler), axis=0)
            wav = jnp.dot(bands[c, 0], near, preferred_element_type=F32)
            wav = wav + jnp.dot(bands[c, 0, :, :rows], own_lo[c], preferred_element_type=F32)
            wav = wav + jnp.dot(bands[c, 1], near, preferred_element_type=F32)
            m_v[c] = m_v[c] - step[c] * wav

    def arrive_a(p):
        k, top, end = pieces[p]
        for g in range(nblk):
            span = 4 * wide
            part = recv_a.at[k, top:end, g * span : (g + 1) * span]
            pltpu.make_async_copy(part, part, a_recv.at[p, g]).wait()
            dirty = jnp.dot(
                recv_a[k, top:end, g * span : (g + 1) * span], tb[4 * g : 4 * g + 4].reshape(span, side),
                preferred_element_type=F32,
            )
            base[k, top:end] = base[k, top:end] + dirty if g else dirty

    def depart_b(p):
        k, top, end = pieces[p]
        value = m_v[k, top:end] + step[k] * base[k, top:end]
        base[k, top:end] = value
        send_b[k, top:end] = value.astype(BF16)
        pltpu.make_async_copy(base.at[k, top:end], moved.at[k, top:end], out_sem).start()
        if end - top == rows:
            for peer in peers:
                b_remote(k, peer).start()
            pltpu.make_async_copy(b_src(k, me_c), recv_b.at[k, me_c], b_recv.at[k]).start()
            return
        core = top // half
        for j in range(0, chans - 2, 2):
            b_remote(k, p_bit[1 - j // 2 % 2] + x_of[xsteps[j // 4]] + core).start()

        @pl.when(rh == core)
        def _():
            pltpu.make_async_copy(b_src(k, me_c), recv_b.at[k, me_c], b_recv.at[k]).start()

        @pl.when(rh != core)
        def _():
            b_remote(k, peers[-1]).start()

    def g_remote(k, peer):
        return pltpu.make_async_remote_copy(
            src_ref=grecv.at[k, me_c], dst_ref=grecv.at[k, me_c], send_sem=g_send, recv_sem=g_recv.at[k],
            device_id=(me_s, peer), device_id_type=MESH,
        )

    def arrive_b(k):
        part = recv_b.at[k]
        pltpu.make_async_copy(part, part, b_recv.at[k]).wait()
        stage[: chans * half, :] = recv_b[k].astype(F32).reshape(chans * half, 128)
        for m in range(half):
            x[k * chans : (k + 1) * chans, m * 128 : (m + 1) * 128] = stage[pl.ds(m, chans, stride=half), :].astype(BF16)
        part = lax.dot_general(x[k * chans : (k + 1) * chans, :], x[...], NT, preferred_element_type=F32)
        grecv[k, me_c] = part[: chans // 2] + pltpu.roll(part[chans // 2 :], size, 1)

        for peer in peers:
            g_remote(k, peer).start()

    last = local - 1
    size = local * chans
    for k in range(last):
        arrive_a(k)
        if k == 1:
            wavelet()
            depart_b(0)
        if k:
            depart_b(k)
    for p in range(last, len(pieces)):
        arrive_a(p)
        depart_b(p)
    for k in range(local):
        arrive_b(k)

    blocks = []
    for k in range(local):
        part = grecv.at[k, : chans - 1]
        pltpu.make_async_copy(part, part, g_recv.at[k]).wait()
        part = jnp.sum(grecv[k], axis=0)
        blocks += [part, pltpu.roll(part, size, 1)]
    low = jnp.concatenate(blocks, axis=0)[:, :size]
    gi = lax.broadcasted_iota(jnp.int32, (size, size), 0)
    gj = lax.broadcasted_iota(jnp.int32, (size, size), 1)
    identity = jnp.where(gi == gj, 1.0, 0.0).astype(F32)
    strict = jnp.where(gi // chans > gj // chans, low, 0.0)
    upper = lax.dot_general(
        strict, identity, (((0,), (0,)), ((), ())), precision=lax.Precision.HIGHEST, preferred_element_type=F32
    )
    gram = low + upper
    square = jnp.sum(jnp.sum(gram * gram, axis=1, keepdims=True), axis=0, keepdims=True)
    frob = jnp.sqrt(square)
    current = gram / frob
    inverse = 0.5 * (3.0 * identity - current)
    current = split_dot(split(current), split(inverse))
    for it in range(1, NS_ITERS):
        parts = split(inverse)
        halves = split(current)
        middle = split(0.5 * (3.0 * identity - split_dot(parts, halves)))
        if it + 1 < NS_ITERS:
            current = split_dot(halves, middle)
        inverse = split_dot(middle, parts)
    mix = (shrink[0] * jnp.sqrt(float(rows * side) / frob) * inverse).astype(BF16)

    quarter = half // 2
    span = chans * quarter
    for h in range(2):
        for q in range(quarter // 4):
            first = (h * quarter + q * 4) * 128
            value = jnp.dot(mix, x[:size, first : first + 512], preferred_element_type=F32)
            for t in range(4):
                stage[pl.ds(q * 4 + t, size, stride=quarter), :] = value[:, t * 128 : (t + 1) * 128]
        for k in range(local):
            send_c[h, :, k] = stage[k * span : (k + 1) * span, :].reshape(chans, quarter, 128).astype(BF16)
        mine = polar.at[
            :, pl.ds(pl.multiple_of(rh * half + h * quarter, quarter), quarter), pl.ds(pl.multiple_of(lb * 128, 128), 128)
        ]

        for peer in peers:
            pltpu.make_async_remote_copy(
                src_ref=send_c.at[h, peer], dst_ref=mine, send_sem=c_send, recv_sem=c_recv,
                device_id=(me_s, peer), device_id_type=MESH,
            ).start()

        pltpu.make_async_copy(send_c.at[h, me_c], mine, c_recv).start()
    pltpu.make_async_copy(base, moved, out_sem).wait()
    pltpu.make_async_copy(polar, polar, c_recv).wait()

    for ref, i in ((halo_out.at[0], 0), (relay, 1), (relay, 2), (relay, 3)):
        pltpu.make_async_copy(ref, ref, h_send.at[i]).wait()
    for ref, sem in (
        (send_a.at[: (strips - 1) * rows], a_send),
        (recv_b.at[:, : chans - 1], b_send),
        (grecv.at[:, : chans - 1], g_send),
        (send_c.at[:, : chans - 1], c_send),
    ):
        pltpu.make_async_copy(ref, ref, sem).wait()


def solution(mesh):
    strips, chans = mesh.shape["strip"], mesh.shape["chan"]

    def step_fn(grid, model, step, taps, shrink):
        local, rows, side = model.shape
        wide = 2 * rows
        half = rows // 2
        reach = (taps.shape[1] - 1) * 2 ** (taps.shape[0] - 1)
        tab = make_tables(side, strips)
        dma = pltpu.SemaphoreType.DMA
        anywhere = pl.BlockSpec(memory_space=pl.ANY)
        scalars = pl.BlockSpec(memory_space=pltpu.SMEM)
        moved, polar = pl.pallas_call(
            functools.partial(kernel, strips, chans),
            out_shape=(
                pltpu.VMEM((local, rows, side), F32),
                pltpu.VMEM((local, rows, side), BF16),
            ),
            in_specs=[anywhere, anywhere, anywhere, scalars, scalars, scalars],
            out_specs=(pl.BlockSpec(memory_space=pltpu.VMEM),) * 2,
            scratch_shapes=[
                pltpu.VMEM((strips, 2, rows, side), BF16),
                pltpu.VMEM((2, local, rows, side), BF16),
                pltpu.VMEM((local, rows, side), F32),
                pltpu.VMEM((local * wide, side), BF16),
                pltpu.VMEM((local * wide, side), BF16),
                pltpu.VMEM((side, local * wide), BF16),
                pltpu.VMEM((local, rows, strips * wide), BF16),
                pltpu.VMEM((local, rows, side), BF16),
                pltpu.VMEM((local, rows, side), BF16),
                pltpu.VMEM((local, rows, side), F32),
                pltpu.VMEM((local, rows, side), BF16),
                pltpu.VMEM((local, chans, half, 128), BF16),
                pltpu.VMEM((128, half * 128), BF16),
                pltpu.VMEM((local, chans, chans // 2, 128), F32),
                pltpu.VMEM((local * chans * half // 2, 128), F32),
                pltpu.VMEM((2, chans, local, half // 2, 128), BF16),
                pltpu.VMEM((local * reach, side // 2), BF16),
                pltpu.VMEM((2, local * reach, side), F32),
                pltpu.VMEM((2, local * reach, side), BF16),
                pltpu.VMEM((2, local * reach, side), BF16),
                pltpu.VMEM((local, 2, rows, 256), BF16),
                dma((2,)), dma((strips // 4,)),
                dma, dma((local + 1, strips // 4)),
                dma, dma((local,)),
                dma, dma((local,)),
                dma, dma,
                dma((4,)), dma((4,)), dma,
            ],
            compiler_params=pltpu.CompilerParams(
                collective_id=0, has_side_effects=True, vmem_limit_bytes=60 * 1024 * 1024
            ),
            name="imaging_step",
        )(tab, grid, model, step, taps, shrink)
        return moved - polar.astype(F32)

    return jax.shard_map(
        step_fn,
        mesh=mesh,
        in_specs=(
            P(None, "chan", "strip", None),
            P("chan", "strip", None),
            P("chan"),
            P(),
            P("strip"),
        ),
        out_specs=P("chan", "strip", None),
        check_vma=False,
    )
```

```python
import functools

import jax
import jax.numpy as jnp
import numpy as np
from jax import lax
from jax.experimental import pallas as pl
from jax.experimental.pallas import tpu as pltpu
from jax.sharding import PartitionSpec as P

NS_ITERS = 5
MESH = pl.DeviceIdType.MESH
NT = (((1,), (1,)), ((), ()))
F32 = jnp.float32
BF16 = jnp.bfloat16


def make_tables(side, strips):
    index = np.arange(side, dtype=np.int64)
    phases = (index[:, None] * index[None, :] % side) * (2.0 * np.pi / side)
    scale = float(side) ** -0.5
    both = np.stack((np.cos(phases), np.sin(phases))) * scale
    both = both.reshape(2, strips, side // strips, side).swapaxes(0, 1)
    return jnp.asarray(both.astype(np.float32).astype(BF16))


def split(a):
    high = a.astype(BF16)
    return high, (a - high.astype(F32)).astype(BF16)


def split_dot(a, b):
    out = jnp.dot(a[0], b[1], preferred_element_type=F32) + jnp.dot(a[1], b[0], preferred_element_type=F32)
    return out + jnp.dot(a[0], b[0], preferred_element_type=F32)


def kernel(
    strips, chans, tab, grid, model, step, taps, shrink, moved, polar,
    tb, g_v, m_v, xc, xs, send_a, recv_a, own_hi, own_lo, base, send_b, recv_b, x, grecv,
    stage, send_c, relay, edge, halo_out, halo_in, bands,
    load_sem, tab_sem, a_send, a_recv, b_send, b_recv, g_send, g_recv, c_send, c_recv, h_send, h_recv, out_sem,
):
    me_s = lax.axis_index("strip")
    me_c = lax.axis_index("chan")
    local, rows, side = base.shape
    wide = 2 * rows
    half = rows // 2
    lb = me_c // 2
    rh = lax.rem(me_c, 2)
    levels, filt = taps.shape
    reach = (filt - 1) * 2 ** (levels - 1)
    ring = strips // 2
    xring = chans // 4

    z_of = [lax.rem(me_s // 2 + d, ring) * 2 for d in range(ring)]
    z_bit = [lax.rem(me_s, 2), 1 - lax.rem(me_s, 2)]
    steps = [(ring // 2 + ((q + 1) // 2) * (1 - 2 * (q % 2))) % ring for q in range(ring)]
    slots = [(-steps[j // 2] % ring, 1 - j % 2) for j in range(strips)]
    strip_of = [z_of[d] + z_bit[t] for d, t in slots]
    partner = [slots.index((-d % ring, t)) for d, t in slots]

    x_of = [lax.rem(me_c // 2 + d, xring) * 2 for d in range(xring)]
    c_bit = [lax.rem(me_c, 2), 1 - lax.rem(me_c, 2)]
    me_pair = me_c // (2 * xring)
    p_bit = [me_pair * (2 * xring), (1 - me_pair) * (2 * xring)]
    xsteps = [(xring // 2 + ((q + 1) // 2) * (1 - 2 * (q % 2))) % xring for q in range(xring)]
    peers = [p_bit[1 - j // 2 % 2] + x_of[xsteps[j // 4]] + c_bit[1 - j % 2] for j in range(chans - 1)]

    def strip_next(d):
        return lax.rem(me_s + d + strips, strips)

    barrier = pltpu.get_barrier_semaphore()

    for j in range(strips - 1):
        pl.semaphore_signal(barrier, inc=1, device_id=(strip_of[j], me_c), device_id_type=MESH)

    load_grid = pltpu.make_async_copy(grid, g_v, load_sem.at[0])
    load_grid.start()

    def tab_start(i):
        for j in range(4 * i, 4 * i + 4):
            pltpu.make_async_copy(tab.at[strip_of[j]], tb.at[j], tab_sem.at[i]).start()

    def tab_wait(i):
        part = tb.at[4 * i : 4 * i + 4]
        pltpu.make_async_copy(part, part, tab_sem.at[i]).wait()

    tab_start(0)

    for peer in peers:
        pl.semaphore_signal(barrier, inc=1, device_id=(me_s, peer), device_id_type=MESH)

    nblk = strips // 4
    for i in range(1, nblk):
        tab_start(i)
    load_model = pltpu.make_async_copy(model, m_v, load_sem.at[1])
    load_model.start()

    load_grid.wait()
    for c in range(local):
        re = g_v[0, c]
        im = -g_v[1, c]
        xc[c * wide : c * wide + rows, :] = re
        xc[c * wide + rows : (c + 1) * wide, :] = im
        xs[c * wide : c * wide + rows, :] = im
        xs[c * wide + rows : (c + 1) * wide, :] = -re

    pieces = [(k, 0, rows) for k in range(local - 1)] + [(local - 1, 0, half), (local - 1, half, rows)]

    def a_src(p, j):
        k, top, end = pieces[p]
        return send_a.at[j * rows + top : j * rows + end, k * wide : (k + 1) * wide]

    def a_dst(p, j):
        k, top, end = pieces[p]
        return recv_a.at[k, top:end, partner[j] * wide : (partner[j] + 1) * wide]

    def a_remote(k, j):
        return pltpu.make_async_remote_copy(
            src_ref=a_src(k, j), dst_ref=a_dst(k, j), send_sem=a_send, recv_sem=a_recv.at[k, partner[j] // 4],
            device_id=(strip_of[j], me_c), device_id_type=MESH,
        )

    def a_local(k):
        last = strips - 1
        return pltpu.make_async_copy(a_src(k, last), a_dst(k, last), a_recv.at[k, nblk - 1])

    for i in range(nblk):
        tab_wait(i)
        cos_rows = tb[4 * i : 4 * i + 4, 0].reshape(4 * rows, side)
        sin_rows = tb[4 * i : 4 * i + 4, 1].reshape(4 * rows, side)
        value = lax.dot_general(cos_rows, xc[...], NT, preferred_element_type=F32)
        value = value + lax.dot_general(sin_rows, xs[...], NT, preferred_element_type=F32)
        send_a[4 * i * rows : 4 * (i + 1) * rows, :] = value.astype(BF16)
        if i == 0:
            pl.semaphore_wait(barrier, strips - 1 + chans - 1)

        for j in range(4 * i, min(4 * i + 4, strips - 1)):
            a_remote(0, j).start()

    a_local(0).start()

    load_model.wait()
    for c in range(local):
        value = m_v[c]
        top = value.astype(BF16)
        own_hi[c] = top
        own_lo[c] = (value - top.astype(F32)).astype(BF16)
        edge[0, c * reach : (c + 1) * reach] = m_v[c, rows - reach :]
        edge[1, c * reach : (c + 1) * reach] = m_v[c, :reach]
    halo_out[...] = edge[...].astype(BF16)
    bit = lax.rem(me_s, 2)
    part = side // 2
    pair = 1 - 2 * bit

    def leg(i, src, dst, to):
        return pltpu.make_async_remote_copy(
            src_ref=src, dst_ref=dst, send_sem=h_send.at[i], recv_sem=h_recv.at[i],
            device_id=(strip_next(to), me_c), device_id_type=MESH,
        )

    legs = [
        leg(0, halo_out.at[bit], halo_in.at[bit], pair),
        leg(1, halo_out.at[1 - bit, :, :part], halo_in.at[1 - bit, :, :part], -pair),
        leg(2, halo_out.at[1 - bit, :, part:], relay, pair),
    ]
    for i in (2, 0, 1):
        legs[i].start()

    for j in range(strips - 1):
        a_remote(1, j).start()
    a_local(1).start()
    legs[2].wait_recv()
    leg(3, relay, halo_in.at[bit, :, part:], 2 * pair).start()
    for k in range(2, local + 1):
        for j in range(strips - 1):
            a_remote(k, j).start()
        a_local(k).start()

    total = strips * rows
    base_row = me_s * rows
    row = lax.broadcasted_iota(jnp.int32, (rows, 256), 0)
    col = lax.broadcasted_iota(jnp.int32, (rows, 256), 1)
    for c in range(local):
        before = col - rows - c * reach
        after = before - local * reach
        own = col < rows
        in_before = jnp.logical_and(before >= 0, before < reach)
        in_after = jnp.logical_and(after >= 0, after < reach)
        place = jnp.where(own, col, jnp.where(in_before, before - reach, rows + after))
        shift = place - row
        band = jnp.zeros((rows, 256), F32)
        for j in range(levels):
            dil = 2**j
            for k in range(filt):
                inner = jnp.zeros((rows, 256), F32)
                for q in range(filt):
                    inner = inner + jnp.where(shift == (q - k) * dil, taps[j, q], 0.0)
                detail_row = base_row + row - (k - filt // 2) * dil
                ok = jnp.logical_and(detail_row >= 0, detail_row < total)
                band = band + jnp.where(ok, taps[j, k] * inner, 0.0)
        image_row = base_row + place
        known = jnp.logical_or(own, jnp.logical_or(in_before, in_after))
        known = jnp.logical_and(known, jnp.logical_and(image_row >= 0, image_row < total))
        band = jnp.where(known, band, 0.0)
        band_hi = band.astype(BF16)
        bands[c, 0] = band_hi
        bands[c, 1] = (band - band_hi.astype(F32)).astype(BF16)
    x[...] = jnp.zeros(x.shape, BF16)
    def b_src(k, peer):
        return send_b.at[
            k, pl.ds(pl.multiple_of(lax.rem(peer, 2) * half, half), half), pl.ds(pl.multiple_of(peer // 2 * 128, 128), 128)
        ]

    def b_remote(k, peer):
        return pltpu.make_async_remote_copy(
            src_ref=b_src(k, peer), dst_ref=recv_b.at[k, me_c], send_sem=b_send, recv_sem=b_recv.at[k],
            device_id=(me_s, peer), device_id_type=MESH,
        )

    def wavelet():
        for ref, i in ((halo_in.at[0], 0), (relay, 1), (relay, 3)):
            pltpu.make_async_copy(ref, ref, h_recv.at[i]).wait()
        filler = jnp.zeros((256 - rows - 2 * local * reach, side), BF16)
        for c in range(local):
            near = jnp.concatenate((own_hi[c], halo_in[0], halo_in[1], filler), axis=0)
            wav = jnp.dot(bands[c, 0], near, preferred_element_type=F32)
            wav = wav + jnp.dot(bands[c, 0, :, :rows], own_lo[c], preferred_element_type=F32)
            wav = wav + jnp.dot(bands[c, 1], near, preferred_element_type=F32)
            m_v[c] = m_v[c] - step[c] * wav

    def arrive_a(p):
        k, top, end = pieces[p]
        for g in range(nblk):
            span = 4 * wide
            part = recv_a.at[k, top:end, g * span : (g + 1) * span]
            pltpu.make_async_copy(part, part, a_recv.at[p, g]).wait()
            dirty = jnp.dot(
                recv_a[k, top:end, g * span : (g + 1) * span], tb[4 * g : 4 * g + 4].reshape(span, side),
                preferred_element_type=F32,
            )
            base[k, top:end] = base[k, top:end] + dirty if g else dirty

    def depart_b(p):
        k, top, end = pieces[p]
        value = m_v[k, top:end] + step[k] * base[k, top:end]
        base[k, top:end] = value
        send_b[k, top:end] = value.astype(BF16)
        pltpu.make_async_copy(base.at[k, top:end], moved.at[k, top:end], out_sem).start()
        if end - top == rows:
            for peer in peers:
                b_remote(k, peer).start()
            pltpu.make_async_copy(b_src(k, me_c), recv_b.at[k, me_c], b_recv.at[k]).start()
            return
        core = top // half
        for j in range(0, chans - 2, 2):
            b_remote(k, p_bit[1 - j // 2 % 2] + x_of[xsteps[j // 4]] + core).start()

        @pl.when(rh == core)
        def _():
            pltpu.make_async_copy(b_src(k, me_c), recv_b.at[k, me_c], b_recv.at[k]).start()

        @pl.when(rh != core)
        def _():
            b_remote(k, peers[-1]).start()

    def g_remote(k, peer):
        return pltpu.make_async_remote_copy(
            src_ref=grecv.at[k, me_c], dst_ref=grecv.at[k, me_c], send_sem=g_send, recv_sem=g_recv.at[k],
            device_id=(me_s, peer), device_id_type=MESH,
        )

    def arrive_b(k):
        part = recv_b.at[k]
        pltpu.make_async_copy(part, part, b_recv.at[k]).wait()
        stage[: chans * half, :] = recv_b[k].astype(F32).reshape(chans * half, 128)
        for m in range(half):
            x[k * chans : (k + 1) * chans, m * 128 : (m + 1) * 128] = stage[pl.ds(m, chans, stride=half), :].astype(BF16)
        part = lax.dot_general(x[k * chans : (k + 1) * chans, :], x[...], NT, preferred_element_type=F32)
        grecv[k, me_c] = part[: chans // 2] + pltpu.roll(part[chans // 2 :], size, 1)

        for peer in peers:
            g_remote(k, peer).start()

    last = local - 1
    size = local * chans
    for k in range(last):
        arrive_a(k)
        if k == 1:
            wavelet()
            depart_b(0)
        if k:
            depart_b(k)
    for p in range(last, len(pieces)):
        arrive_a(p)
        depart_b(p)
    for k in range(local):
        arrive_b(k)

    blocks = []
    for k in range(local):
        part = grecv.at[k, : chans - 1]
        pltpu.make_async_copy(part, part, g_recv.at[k]).wait()
        part = jnp.sum(grecv[k], axis=0)
        blocks += [part, pltpu.roll(part, size, 1)]
    low = jnp.concatenate(blocks, axis=0)[:, :size]
    gi = lax.broadcasted_iota(jnp.int32, (size, size), 0)
    gj = lax.broadcasted_iota(jnp.int32, (size, size), 1)
    identity = jnp.where(gi == gj, 1.0, 0.0).astype(F32)
    strict = jnp.where(gi // chans > gj // chans, low, 0.0)
    upper = lax.dot_general(
        strict, identity, (((0,), (0,)), ((), ())), precision=lax.Precision.HIGHEST, preferred_element_type=F32
    )
    gram = low + upper
    square = jnp.sum(jnp.sum(gram * gram, axis=1, keepdims=True), axis=0, keepdims=True)
    frob = jnp.sqrt(square)
    current = gram / frob
    inverse = 0.5 * (3.0 * identity - current)
    current = split_dot(split(current), split(inverse))
    for it in range(1, NS_ITERS):
        parts = split(inverse)
        halves = split(current)
        middle = split(0.5 * (3.0 * identity - split_dot(parts, halves)))
        if it + 1 < NS_ITERS:
            current = split_dot(halves, middle)
        inverse = split_dot(middle, parts)
    mix = (shrink[0] * jnp.sqrt(float(rows * side) / frob) * inverse).astype(BF16)

    quarter = half // 2
    span = chans * quarter
    for h in range(2):
        for q in range(quarter // 4):
            first = (h * quarter + q * 4) * 128
            value = jnp.dot(mix, x[:size, first : first + 512], preferred_element_type=F32)
            for t in range(4):
                stage[pl.ds(q * 4 + t, size, stride=quarter), :] = value[:, t * 128 : (t + 1) * 128]
        for k in range(local):
            send_c[h, :, k] = stage[k * span : (k + 1) * span, :].reshape(chans, quarter, 128).astype(BF16)
        mine = polar.at[
            :, pl.ds(pl.multiple_of(rh * half + h * quarter, quarter), quarter), pl.ds(pl.multiple_of(lb * 128, 128), 128)
        ]

        for peer in peers:
            pltpu.make_async_remote_copy(
                src_ref=send_c.at[h, peer], dst_ref=mine, send_sem=c_send, recv_sem=c_recv,
                device_id=(me_s, peer), device_id_type=MESH,
            ).start()

        pltpu.make_async_copy(send_c.at[h, me_c], mine, c_recv).start()
    pltpu.make_async_copy(base, moved, out_sem).wait()
    pltpu.make_async_copy(polar, polar, c_recv).wait()

    for ref, i in ((halo_out.at[0], 0), (relay, 1), (relay, 2), (relay, 3)):
        pltpu.make_async_copy(ref, ref, h_send.at[i]).wait()
    for ref, sem in (
        (send_a.at[: (strips - 1) * rows], a_send),
        (recv_b.at[:, : chans - 1], b_send),
        (grecv.at[:, : chans - 1], g_send),
        (send_c.at[:, : chans - 1], c_send),
    ):
        pltpu.make_async_copy(ref, ref, sem).wait()


def solution(mesh):
    strips, chans = mesh.shape["strip"], mesh.shape["chan"]

    def step_fn(grid, model, step, taps, shrink):
        local, rows, side = model.shape
        wide = 2 * rows
        half = rows // 2
        reach = (taps.shape[1] - 1) * 2 ** (taps.shape[0] - 1)
        tab = make_tables(side, strips)
        dma = pltpu.SemaphoreType.DMA
        anywhere = pl.BlockSpec(memory_space=pl.ANY)
        scalars = pl.BlockSpec(memory_space=pltpu.SMEM)
        moved, polar = pl.pallas_call(
            functools.partial(kernel, strips, chans),
            out_shape=(
                pltpu.VMEM((local, rows, side), F32),
                pltpu.VMEM((local, rows, side), BF16),
            ),
            in_specs=[anywhere, anywhere, anywhere, scalars, scalars, scalars],
            out_specs=(pl.BlockSpec(memory_space=pltpu.VMEM),) * 2,
            scratch_shapes=[
                pltpu.VMEM((strips, 2, rows, side), BF16),
                pltpu.VMEM((2, local, rows, side), BF16),
                pltpu.VMEM((local, rows, side), F32),
                pltpu.VMEM((local * wide, side), BF16),
                pltpu.VMEM((local * wide, side), BF16),
                pltpu.VMEM((side, local * wide), BF16),
                pltpu.VMEM((local, rows, strips * wide), BF16),
                pltpu.VMEM((local, rows, side), BF16),
                pltpu.VMEM((local, rows, side), BF16),
                pltpu.VMEM((local, rows, side), F32),
                pltpu.VMEM((local, rows, side), BF16),
                pltpu.VMEM((local, chans, half, 128), BF16),
                pltpu.VMEM((128, half * 128), BF16),
                pltpu.VMEM((local, chans, chans // 2, 128), F32),
                pltpu.VMEM((local * chans * half // 2, 128), F32),
                pltpu.VMEM((2, chans, local, half // 2, 128), BF16),
                pltpu.VMEM((local * reach, side // 2), BF16),
                pltpu.VMEM((2, local * reach, side), F32),
                pltpu.VMEM((2, local * reach, side), BF16),
                pltpu.VMEM((2, local * reach, side), BF16),
                pltpu.VMEM((local, 2, rows, 256), BF16),
                dma((2,)), dma((strips // 4,)),
                dma, dma((local + 1, strips // 4)),
                dma, dma((local,)),
                dma, dma((local,)),
                dma, dma,
                dma((4,)), dma((4,)), dma,
            ],
            compiler_params=pltpu.CompilerParams(
                collective_id=0, has_side_effects=True, vmem_limit_bytes=60 * 1024 * 1024
            ),
            name="imaging_step",
        )(tab, grid, model, step, taps, shrink)
        return moved - polar.astype(F32)

    return jax.shard_map(
        step_fn,
        mesh=mesh,
        in_specs=(
            P(None, "chan", "strip", None),
            P("chan", "strip", None),
            P("chan"),
            P(),
            P("strip"),
        ),
        out_specs=P("chan", "strip", None),
        check_vma=False,
    )
```
